32 devices in a mesh: seq: 4 (over z), head: 4 (over y, x), rep: 2 (over core).
Axes of the slice: x: 2, y: 2, z: 4, core: 2. Of those that a mesh axis runs over, the one named last changes fastest.
Arguments:
- moe_in: bfloat16 [1024, 2048], P(('rep', 'seq'), 'head'), parts along dimension 0, may hold values from -6 to 6
- grad_out: bfloat16 [1024, 2048], P(('rep', 'seq'), 'head'), parts along dimension 0, may hold values from -6 to 6
- routes: int32 [1024, 8], P(('rep', 'seq')), parts along dimension 0, may hold values from 0 to 63, all different within a row; in each aligned block of 128 rows (0 to 127, 128 to 255, ...) at most 18 rows name the same one
- route_weight: bfloat16 [1024, 8], P(('rep', 'seq')), parts along dimension 0, may hold values from 0.049804688 to 0.5
- w_gate: bfloat16 [64, 2048, 512], P('seq', None, 'head'), may hold values from -0.125 to 0.125
- w_up: bfloat16 [64, 2048, 512], P('seq', None, 'head'), may hold values from -0.125 to 0.125
- w_down: bfloat16 [64, 512, 2048], P('seq', 'head'), may hold values from -0.25 to 0.25
- queries: bfloat16 [1024, 2048], P(('rep', 'seq'), 'head'), parts along dimension 0, may hold values from -8 to 8
- key_value: bfloat16 [1024, 4, 128], P(('rep', 'seq'), 'head'), parts along dimension 0, may hold values from -8 to 8
Outputs:
- d_moe_in: bfloat16 [1024, 2048], P(('rep', 'seq'), 'head'), parts along dimension 0
- d_route_weight: bfloat16 [1024, 8], P(('rep', 'seq')), parts along dimension 0
- grad_gate: bfloat16 [128, 2048, 512], P(('rep', 'seq'), None, 'head'), parts along dimension 0
- grad_up: bfloat16 [128, 2048, 512], P(('rep', 'seq'), None, 'head'), parts along dimension 0
- grad_down: bfloat16 [128, 512, 2048], P(('rep', 'seq'), 'head'), parts along dimension 0
- d_queries: bfloat16 [1024, 2048], P(('rep', 'seq'), 'head'), parts along dimension 0
- d_key_value: bfloat16 [1024, 4, 128], P(('rep', 'seq'), 'head'), parts along dimension 0
The draws below stay inside these ranges and needn't reach their ends.
There are 2 independent parts, one for each index of `rep`. The reference program is written for one: setup_inputs(seed, part) draws one part's arguments, and reference() takes and returns one part's arrays. A program takes and returns all parts, laid end to end along the dimension named above; an argument that names none is the same for every part. Nothing has to cross between parts.
Inputs may be any that keep to these rules, and one draw needn't show every extreme that they name: `routes`: each row names 8 different experts. In each aligned block of 128 rows (the tokens of one sequence shard) no expert is named by more than 18 rows, and in every draw some block has an expert named by exactly 18 rows.
All inputs are finite; a program needn't handle non-finite values.
Results may differ from the reference program's by a relative error of at most 0.03.
Values may be sent and summed in bfloat16 or wider, within the bound.
A program may use at most 128 MiB of HBM per device.

```python
import math
import jax
import jax.numpy as jnp
import numpy as np
from jax import lax

TOK_DEV = 128
D = 2048
HEADS = 32
KVH = 4
HD = 64
FF = 512
EXPERTS = 64
TOPK = 8
WIN = 512
CAP = 18
TOKENS = 512
N_HEAD = 4


def attention_inputs(key):
    base = jax.random.fold_in(key, 4242)
    key_q, key_k, key_v = jax.random.split(base, 3)
    width_q = HEADS * HD
    query_all = jax.random.truncated_normal(key_q, -4.0, 4.0, (TOKENS, width_q), jnp.float32)
    key_all = jax.random.truncated_normal(key_k, -4.0, 4.0, (TOKENS, KVH, HD), jnp.float32)
    value_all = jax.random.truncated_normal(key_v, -4.0, 4.0, (TOKENS, KVH, HD), jnp.float32)
    return (query_all, jnp.concatenate([key_all, value_all], axis=2))


def draw_queries(key, part):
    return attention_inputs(key)[0].astype(jnp.bfloat16)


def draw_key_value(key, part):
    return attention_inputs(key)[1].astype(jnp.bfloat16)


def block_scale(own_key, shape, cuts, smallest, largest):
    factor_of, own = 1.0, jax.random.fold_in(own_key, 6)
    for dim, parts in cuts:
        heights = jnp.exp(jax.random.uniform(jax.random.fold_in(own, dim), (parts,), jnp.float32, smallest / len(cuts), largest / len(cuts)))
        factor_of = factor_of * jnp.repeat(heights, shape[dim] // parts).reshape([-1 if axis == dim else 1 for axis in range(len(shape))])
    return factor_of


def deal_out(own_key, own, number, rows, count, top, bound, slope):
    sequence = jax.random.permutation(own_key, count)
    crowded, ordinary = shares(count, rows * top, bound, slope, True), shares(count, rows * top, bound, slope, False)
    places = jnp.arange(count)

    def named(lengths, offset_by):
        used = int((lengths > 0).sum())
        fixed = max(1, used // 4)
        moved = fixed + (places - fixed + offset_by * (used - fixed)) % max(1, count - fixed)
        return jnp.zeros((count,), jnp.int32).at[sequence[jnp.where(places < fixed, places, moved)]].set(jnp.asarray(lengths, jnp.int32))

    lengths = jnp.where(number % 4 == 0, named(crowded, number // 4), named(ordinary, number - number // 4 - 1))
    mixed = jax.random.permutation(jax.random.fold_in(own, 3), count)
    giver, taker = mixed[0:count // 2 * 2:2], mixed[1:count // 2 * 2:2]
    margin = jnp.minimum(lengths[giver] - 1, bound - lengths[taker]) // 2
    margin = jnp.where((giver == sequence[0]) | (taker == sequence[0]) | (lengths[taker] == 0), 0, jnp.maximum(margin, 0))
    moved = jax.random.randint(jax.random.fold_in(own, 4), (count // 2,), 0, 1 << 20) % (margin + 1)
    lengths = lengths.at[giver].add(-moved).at[taker].add(moved)
    labels = jnp.searchsorted(jnp.cumsum(lengths), jnp.arange(rows * top), side="right").astype(jnp.int32)
    listing = labels.reshape(top, rows).T
    listing = listing[jax.random.permutation(jax.random.fold_in(own, 1), rows)]
    offset_by = jax.random.randint(jax.random.fold_in(own, 2), (rows, 1), 0, top)
    return jnp.take_along_axis(listing, (jnp.arange(top)[None, :] + offset_by) % top, axis=1)


def shares(amount, total, limit, skew, full):
    weights = [(1 << 20) // math.isqrt(standing ** skew) + 1 for standing in range(1, amount + 1)]
    largest = limit if full else min(limit, max(-(-total // amount), total * weights[0] // sum(weights)))
    least = 1 if total - largest >= amount - 1 else 0
    counts, spare = [largest] + [least] * (amount - 1), total - largest - least * (amount - 1)
    while spare > 0:
        candidates = [i for i in range(1, amount) if counts[i] < largest] or [i for i in range(1, amount) if counts[i] < limit]
        whole, remaining = sum([weights[i] for i in candidates]), spare
        for i in candidates:
            more = min(limit - counts[i], max(1, remaining * weights[i] // whole), spare)
            counts[i] = counts[i] + more
            spare = spare - more
    return np.array(counts)


def normal_values(own_key, shape, spread, limit, shards=(), kind=jnp.bfloat16):
    values = jax.random.normal(own_key, shape, jnp.float32) * spread
    if len(shards) > 0:
        values = block_scale(own_key, shape, shards, -0.22, 0.18) * values
    return jnp.clip(values, min=-limit, max=limit).astype(kind)


def setup_inputs(seed: int = 0, part: int = 0) -> dict:
    streams_of = jax.random.split(jax.random.key(seed), 10)
    part_splits = jax.random.split(jax.random.fold_in(streams_of[9], part), 10)
    moe_in = normal_values(part_splits[0], (TOKENS, D), 1.0, 6.0, ((0, 4), (1, 4)))
    grad_out = normal_values(part_splits[1], (TOKENS, D), 1.0, 6.0, ((0, 4), (1, 4)))
    routes_keys = jax.random.split(jax.random.fold_in(part_splits[2], 1), TOKENS // TOK_DEV)
    routes_turns = jax.random.permutation(jax.random.fold_in(part_splits[2], 3), TOKENS // TOK_DEV)
    routes = jax.vmap(lambda own, number: deal_out(jax.random.fold_in(part_splits[2], 2), own, number, TOK_DEV, EXPERTS, TOPK, CAP, 2))(routes_keys, routes_turns).reshape((TOKENS, TOPK))
    route_weight = jnp.clip(jnp.exp(math.log(0.5) - 2.306499 * jax.random.uniform(part_splits[3], (TOKENS, TOPK), jnp.float32) ** block_scale(part_splits[3], (TOKENS, TOPK), ((0, 4),), -0.2, 0.2)), 0.049804688, 0.5).astype(jnp.bfloat16)
    w_gate = normal_values(streams_of[4], (EXPERTS, D, FF), D ** -0.5, 0.125, ((0, 4), (2, 4)))
    w_up = normal_values(streams_of[5], (EXPERTS, D, FF), D ** -0.5, 0.125, ((0, 4), (2, 4)))
    w_down = normal_values(streams_of[6], (EXPERTS, FF, D), FF ** -0.5, 0.25, ((0, 4), (1, 4)))
    queries = draw_queries(jax.random.fold_in(jax.random.fold_in(streams_of[9], part), 71), part)
    key_value = draw_key_value(jax.random.fold_in(jax.random.fold_in(streams_of[9], part), 71), part)
    return {"moe_in": moe_in, "grad_out": grad_out, "routes": routes, "route_weight": route_weight, "w_gate": w_gate, "w_up": w_up, "w_down": w_down, "queries": queries, "key_value": key_value}


def expert_pass(gate_w, up_w, down_w, rows_in, rows_grad, slot_weight):
    gate_pre = jnp.dot(rows_in, gate_w, preferred_element_type=jnp.float32)
    up_pre = jnp.dot(rows_in, up_w, preferred_element_type=jnp.float32)
    back_proj = jnp.dot(rows_grad, down_w.T, preferred_element_type=jnp.float32)
    sigmoid_gate = jax.nn.sigmoid(gate_pre)
    silu_gate = gate_pre * sigmoid_gate
    active = silu_gate * up_pre
    route_part = jnp.sum(active * back_proj, axis=1).astype(jnp.bfloat16)
    scale_w = slot_weight.astype(jnp.float32)[:, None]
    d_active = scale_w * back_proj
    d_gate = (d_active * up_pre * sigmoid_gate * (1.0 + gate_pre * (1.0 - sigmoid_gate))).astype(jnp.bfloat16)
    d_up = (d_active * silu_gate).astype(jnp.bfloat16)
    weighted = (scale_w * active).astype(jnp.bfloat16)
    slot_count, hidden = d_gate.shape
    width = gate_w.shape[0]
    group_size = hidden // N_HEAD
    partial_value = jnp.einsum("rgf,dgf->grd", d_gate.astype(jnp.float32).reshape(slot_count, N_HEAD, group_size),
                         gate_w.astype(jnp.float32).reshape(width, N_HEAD, group_size))
    partial_value = partial_value + jnp.einsum("rgf,dgf->grd", d_up.astype(jnp.float32).reshape(slot_count, N_HEAD, group_size),
                                   up_w.astype(jnp.float32).reshape(width, N_HEAD, group_size))
    partial_low = lax.optimization_barrier(partial_value.astype(jnp.bfloat16))
    rows_back = jnp.sum(partial_low.astype(jnp.float32), axis=0).astype(jnp.bfloat16)
    grad_gate = jnp.dot(rows_in.T, d_gate, preferred_element_type=jnp.float32).astype(jnp.bfloat16)
    grad_up = jnp.dot(rows_in.T, d_up, preferred_element_type=jnp.float32).astype(jnp.bfloat16)
    grad_down = jnp.dot(weighted.T, rows_grad, preferred_element_type=jnp.float32).astype(jnp.bfloat16)
    return rows_back, route_part, grad_gate, grad_up, grad_down


def reference(moe_in, grad_out, routes, route_weight, w_gate, w_up, w_down, queries, key_value):
    total, top_count = routes.shape
    blocks = total // TOK_DEV
    per_block = TOK_DEV * top_count
    flat_expert = routes.reshape(blocks, per_block)
    one_hot = (flat_expert[:, :, None] == jnp.arange(EXPERTS, dtype=jnp.int32)[None, None, :]).astype(jnp.int32)
    earlier = jnp.cumsum(one_hot, axis=1) - one_hot
    target = (flat_expert * CAP + jnp.sum(earlier * one_hot, axis=2)).astype(jnp.int32)
    block_ids = jnp.broadcast_to(jnp.arange(blocks, dtype=jnp.int32)[:, None], (blocks, per_block))
    pick_ids = jnp.broadcast_to(jnp.arange(per_block, dtype=jnp.int32)[None, :], (blocks, per_block))
    table = jnp.full((blocks, EXPERTS * CAP), per_block, dtype=jnp.int32).at[block_ids, target].set(pick_ids)
    live = table < per_block
    global_pick = (jnp.arange(blocks, dtype=jnp.int32)[:, None] * per_block + jnp.minimum(table, per_block - 1)).astype(jnp.int32)
    token_index = (global_pick // top_count).astype(jnp.int32)

    def by_expert(values):
        return jnp.transpose(values.reshape(blocks, EXPERTS, CAP), (1, 0, 2)).reshape(EXPERTS, blocks * CAP)

    live_e = by_expert(live)
    token_e = by_expert(token_index)
    pick_e = by_expert(global_pick)
    weight_e = jnp.where(live_e, route_weight.reshape(total * top_count)[pick_e], jnp.zeros((), route_weight.dtype))

    def one_expert(inputs):
        gate_w, up_w, down_w, tokens_of, live_of, weight_of = inputs
        rows_in = jnp.where(live_of[:, None], moe_in[tokens_of], jnp.zeros((), moe_in.dtype))
        rows_grad = jnp.where(live_of[:, None], grad_out[tokens_of], jnp.zeros((), grad_out.dtype))
        return expert_pass(gate_w, up_w, down_w, rows_in, rows_grad, weight_of)

    rows_back, route_part, grad_gate, grad_up, grad_down = lax.map(
        one_expert, (w_gate, w_up, w_down, token_e, live_e, weight_e))
    live_flat = live_e.reshape(EXPERTS * blocks * CAP)
    d_moe = jnp.zeros((total, D), jnp.float32).at[token_e.reshape(-1)].add(
        jnp.where(live_flat[:, None], rows_back.reshape(EXPERTS * blocks * CAP, D).astype(jnp.float32), 0.0))
    d_moe_in = d_moe.astype(jnp.bfloat16)
    d_route = jnp.zeros((total * top_count,), jnp.float32).at[pick_e.reshape(-1)].add(
        jnp.where(live_flat, route_part.reshape(-1).astype(jnp.float32), 0.0))
    d_route_weight = d_route.astype(jnp.bfloat16).reshape(total, top_count)

    per_group = HEADS // KVH
    d_hidden = (grad_out.astype(jnp.float32) + d_moe_in.astype(jnp.float32)).astype(jnp.bfloat16)
    kv_padded = jnp.concatenate([jnp.zeros((WIN, KVH, 2 * HD), key_value.dtype), key_value], axis=0)
    query_blocks = queries.reshape(blocks, TOK_DEV, KVH, per_group, HD)
    grad_blocks = d_hidden.reshape(blocks, TOK_DEV, KVH, per_group, HD)
    scale = HD ** -0.5
    length = WIN + TOK_DEV

    def step(carry, inputs):
        query_blk, grad_blk, index = inputs
        start = (index * TOK_DEV).astype(jnp.int32)
        window = lax.dynamic_slice_in_dim(kv_padded, start, length, 0)
        key_rows = window[:, :, :HD].astype(jnp.float32)
        value_rows = window[:, :, HD:].astype(jnp.float32)
        query_f = query_blk.astype(jnp.float32)
        grad_f = grad_blk.astype(jnp.float32)
        scores = jnp.einsum("tghd,jgd->gthj", query_f, key_rows) * scale
        position = start + jnp.arange(TOK_DEV, dtype=jnp.int32)
        key_pos = start - WIN + jnp.arange(length, dtype=jnp.int32)
        visible = (key_pos[None, :] >= 0) & (key_pos[None, :] <= position[:, None]) & (key_pos[None, :] > position[:, None] - WIN)
        scores = jnp.where(visible[None, :, None, :], scores, -1e30)
        row_max = jnp.max(scores, axis=3, keepdims=True)
        raised = jnp.exp(scores - row_max)
        probs = raised / jnp.sum(raised, axis=3, keepdims=True)
        d_probs = jnp.einsum("tghd,jgd->gthj", grad_f, value_rows)
        row_dot = jnp.sum(probs * d_probs, axis=3, keepdims=True)
        d_scores = (probs * (d_probs - row_dot) * scale).astype(jnp.bfloat16).astype(jnp.float32)
        probs_low = probs.astype(jnp.bfloat16).astype(jnp.float32)
        d_query = jnp.einsum("gthj,jgd->tghd", d_scores, key_rows).astype(jnp.bfloat16)
        d_keys = jnp.einsum("gthj,tghd->jgd", d_scores, query_f)
        d_values = jnp.einsum("gthj,tghd->jgd", probs_low, grad_f)
        d_window = jnp.concatenate([d_keys, d_values], axis=2)
        current = lax.dynamic_slice_in_dim(carry, start, length, 0)
        carry = lax.dynamic_update_slice_in_dim(carry, current + d_window, start, 0)
        return carry, d_query

    carry_start = jnp.zeros((WIN + total, KVH, 2 * HD), jnp.float32)
    carry_end, d_query_blocks = lax.scan(step, carry_start, (query_blocks, grad_blocks, jnp.arange(blocks, dtype=jnp.int32)))
    d_queries = d_query_blocks.reshape(total, HEADS * HD)
    d_key_value = carry_end[WIN:].astype(jnp.bfloat16)
    return d_moe_in, d_route_weight, grad_gate, grad_up, grad_down, d_queries, d_key_value
```

```python
import jax
import jax.numpy as jnp
from jax import lax
from jax.experimental import pallas as pl
from jax.experimental.pallas import tpu as pltpu
from jax.sharding import PartitionSpec as P

EXPERTS = 64
WIN = 512
CAP = 18


def shifted(block, axis, distance):
    devices = range(lax.axis_size(axis))
    route = [(i - distance, i) for i in devices if i - distance in devices]
    return lax.ppermute(block, axis, route)


def slot_tables(routes, route_weight):
    token_rows, top_count = routes.shape
    flat_expert = routes.reshape(token_rows * top_count)
    expert_ids = jnp.arange(EXPERTS, dtype=jnp.int32)
    one_hot = (flat_expert[:, None] == expert_ids[None, :]).astype(jnp.int32)
    earlier = jnp.cumsum(one_hot, axis=0) - one_hot
    slot_rank = jnp.sum(earlier * one_hot, axis=1)
    target = flat_expert * CAP + slot_rank
    slot_cells = jnp.arange(EXPERTS * CAP, dtype=jnp.int32)
    chosen = (target[None, :] == slot_cells[:, None]).astype(jnp.float32)
    by_token = jnp.sum(chosen.reshape(EXPERTS * CAP, token_rows, top_count), axis=2).astype(
        jnp.bfloat16
    )
    slot_weight = jnp.dot(
        chosen,
        route_weight.reshape(token_rows * top_count).astype(jnp.float32),
        precision=lax.Precision.HIGHEST,
    )
    return (chosen, by_token, slot_weight.astype(jnp.bfloat16).reshape(EXPERTS, CAP))


def place_rows(by_token, source):
    placed = jnp.dot(by_token, source, preferred_element_type=jnp.float32)
    return placed.astype(jnp.bfloat16).reshape(EXPERTS, CAP, source.shape[1])


def fetch_window(own_rows, reach):
    earlier_shards = [shifted(own_rows, "seq", offset) for offset in range(reach, 0, -1)]
    window = jnp.concatenate(earlier_shards + [own_rows], axis=0)
    return window


def return_window(d_window, reach, shard):
    summed = d_window[reach * shard :]
    for offset in range(1, reach + 1):
        begin = (reach - offset) * shard
        summed = summed + shifted(
            d_window[begin : begin + shard].astype(jnp.bfloat16), "seq", -offset
        ).astype(jnp.float32)
    return summed


def dispatched_experts(moe_in, grad_out, routes, route_weight, w_gate, w_up, w_down):
    seq_count = lax.axis_size("seq")
    local_experts = w_gate.shape[0]
    chosen, by_token, slot_weight = slot_tables(routes, route_weight)
    part_in, part_grad, got_weight = (
        lax.all_to_all(
            place_rows(by_token, moe_in), "seq", split_axis=0, concat_axis=0, tiled=True
        ),
        lax.all_to_all(
            place_rows(by_token, grad_out), "seq", split_axis=0, concat_axis=0, tiled=True
        ),
        lax.all_to_all(slot_weight, "seq", split_axis=0, concat_axis=0, tiled=True),
    )
    got_in, got_grad = (
        lax.all_gather(part_in, "head", axis=2, tiled=True),
        lax.all_gather(part_grad, "head", axis=2, tiled=True),
    )
    width = got_in.shape[2]
    rows_in = got_in.reshape(seq_count, local_experts, CAP, width)
    rows_grad = got_grad.reshape(seq_count, local_experts, CAP, width)
    scale_w = got_weight.reshape(seq_count, local_experts, CAP).astype(jnp.float32)[..., None]
    gate_pre = jnp.einsum("secd,edf->secf", rows_in, w_gate, preferred_element_type=jnp.float32)
    up_pre = jnp.einsum("secd,edf->secf", rows_in, w_up, preferred_element_type=jnp.float32)
    back_proj = jnp.einsum("secd,efd->secf", rows_grad, w_down, preferred_element_type=jnp.float32)
    sigmoid_gate = jax.nn.sigmoid(gate_pre)
    silu_gate = gate_pre * sigmoid_gate
    active = silu_gate * up_pre
    route_part = jnp.sum(active * back_proj, axis=3)
    d_active = scale_w * back_proj
    d_gate = (d_active * up_pre * sigmoid_gate * (1.0 + gate_pre * (1.0 - sigmoid_gate))).astype(
        jnp.bfloat16
    )
    d_up = (d_active * silu_gate).astype(jnp.bfloat16)
    weighted = (scale_w * active).astype(jnp.bfloat16)
    rows_back = jnp.einsum("secf,edf->secd", d_gate, w_gate, preferred_element_type=jnp.float32)
    rows_back = rows_back + jnp.einsum(
        "secf,edf->secd", d_up, w_up, preferred_element_type=jnp.float32
    )
    rows_quarter = lax.psum_scatter(
        rows_back.reshape(seq_count * local_experts, CAP, width).astype(jnp.bfloat16),
        "head",
        scatter_dimension=2,
        tiled=True,
    )
    route_sum = lax.psum(route_part, "head").astype(jnp.bfloat16)
    grad_gate = jnp.einsum(
        "secd,secf->edf", rows_in, d_gate, preferred_element_type=jnp.float32
    ).astype(jnp.bfloat16)
    grad_up = jnp.einsum(
        "secd,secf->edf", rows_in, d_up, preferred_element_type=jnp.float32
    ).astype(jnp.bfloat16)
    grad_down = jnp.einsum(
        "secf,secd->efd", weighted, rows_grad, preferred_element_type=jnp.float32
    ).astype(jnp.bfloat16)
    back_rows, back_weight = (
        lax.all_to_all(rows_quarter, "seq", split_axis=0, concat_axis=0, tiled=True),
        lax.all_to_all(
            route_sum.reshape(seq_count * local_experts, CAP),
            "seq",
            split_axis=0,
            concat_axis=0,
            tiled=True,
        ),
    )
    quarter = back_rows.shape[2]
    d_moe_in = jnp.einsum(
        "st,sd->td",
        by_token,
        back_rows.reshape(EXPERTS * CAP, quarter),
        preferred_element_type=jnp.float32,
    ).astype(jnp.bfloat16)
    d_route = jnp.dot(
        back_weight.reshape(EXPERTS * CAP).astype(jnp.float32),
        chosen,
        precision=lax.Precision.HIGHEST,
    )
    d_route_weight = d_route.astype(jnp.bfloat16).reshape(routes.shape)
    return (d_moe_in, d_route_weight, grad_gate, grad_up, grad_down)


def attention(grad_out, d_moe_in, queries, key_value):
    tokens = grad_out.shape[0]
    head_dim = key_value.shape[2] // 2
    per_group = queries.shape[1] // head_dim
    reach = min(WIN // tokens, lax.axis_size("seq") - 1)
    scale = head_dim ** (-0.5)
    d_hidden = (grad_out.astype(jnp.float32) + d_moe_in.astype(jnp.float32)).astype(jnp.bfloat16)
    query_rows = queries.reshape(tokens * per_group, head_dim)
    grad_rows = d_hidden.reshape(tokens * per_group, head_dim)
    own_rows = key_value.reshape(tokens, 2 * head_dim)
    window = fetch_window(own_rows, reach)
    key_rows = window[:, :head_dim]
    value_rows = window[:, head_dim:]
    contract_last = (((1,), (1,)), ((), ()))
    contract_first = (((0,), (0,)), ((), ()))
    seq_index = lax.axis_index("seq")
    key_pos = (seq_index - reach) * tokens + jnp.arange((reach + 1) * tokens, dtype=jnp.int32)
    row_total = tokens * per_group
    block_rows = min(512, row_total)
    block_count = row_total // block_rows

    def attend_block(index, carry):
        d_window, d_query_all = carry
        begin = (index * block_rows).astype(jnp.int32)
        query_blk = lax.dynamic_slice_in_dim(query_rows, begin, block_rows, 0)
        grad_blk = lax.dynamic_slice_in_dim(grad_rows, begin, block_rows, 0)
        scores = (
            lax.dot_general(query_blk, key_rows, contract_last, preferred_element_type=jnp.float32)
            * scale
        )
        position = (
            seq_index * tokens + (begin + jnp.arange(block_rows, dtype=jnp.int32)) // per_group
        )
        visible = (
            (key_pos[None, :] >= 0)
            & (key_pos[None, :] <= position[:, None])
            & (key_pos[None, :] > position[:, None] - WIN)
        )
        scores = jnp.where(visible, scores, -1e30)
        row_max = jnp.max(scores, axis=1, keepdims=True)
        raised = jnp.exp(scores - row_max)
        probs = raised / jnp.sum(raised, axis=1, keepdims=True)
        d_probs = lax.dot_general(
            grad_blk, value_rows, contract_last, preferred_element_type=jnp.float32
        )
        row_dot = jnp.sum(probs * d_probs, axis=1, keepdims=True)
        d_scores = (probs * (d_probs - row_dot) * scale).astype(jnp.bfloat16)
        probs_low = probs.astype(jnp.bfloat16)
        d_query_blk = jnp.dot(d_scores, key_rows, preferred_element_type=jnp.float32).astype(
            jnp.bfloat16
        )
        d_keys = lax.dot_general(
            d_scores, query_blk, contract_first, preferred_element_type=jnp.float32
        )
        d_values = lax.dot_general(
            probs_low, grad_blk, contract_first, preferred_element_type=jnp.float32
        )
        d_window = d_window + jnp.concatenate([d_keys, d_values], axis=1)
        d_query_all = lax.dynamic_update_slice_in_dim(d_query_all, d_query_blk, begin, 0)
        return (d_window, d_query_all)

    window_start = jnp.zeros(((reach + 1) * tokens, 2 * head_dim), jnp.float32)
    query_start = jnp.zeros((row_total, head_dim), jnp.bfloat16)
    d_window, d_query_all = lax.fori_loop(0, block_count, attend_block, (window_start, query_start))
    d_queries = d_query_all.reshape(tokens, per_group * head_dim)
    d_own = return_window(d_window, reach, tokens)
    d_key_value = d_own.astype(jnp.bfloat16).reshape(tokens, 1, 2 * head_dim)
    return (d_queries, d_key_value)


def dot(a, b, contract):
    return lax.dot_general(a, b, (contract, ((), ())), preferred_element_type=jnp.float32)


def expert_kernel(
    routes_ref,
    weight_ref,
    x_ref,
    dy_ref,
    wg_ref,
    wu_ref,
    wd_ref,
    gg_ref,
    gu_ref,
    gd_ref,
    dmoe_ref,
    droute_ref,
    rank_ref,
    dense_ref,
    pick_ref,
    back_ref,
):
    expert = pl.program_id(0)
    experts = pl.num_programs(0)
    heads, total, quarter = x_ref.shape
    hidden = wg_ref.shape[2]
    rows = pick_ref.shape[0] // rank_ref.shape[0]
    local = rank_ref.shape[0]

    @pl.when(expert == 0)
    def _():
        for index in range(local):
            hit = routes_ref[...] == index
            named = jnp.sum(hit.astype(jnp.float32), axis=0, keepdims=True)
            rank_ref[pl.ds(index, 1), :] = named
            dense_ref[pl.ds(index, 1), :] = jnp.sum(
                jnp.where(hit, weight_ref[...], 0.0), axis=0, keepdims=True
            )
        named = rank_ref[...]
        before = lax.broadcasted_iota(jnp.int32, (total, total), 0)
        after = lax.broadcasted_iota(jnp.int32, (total, total), 1)
        order = (before < after).astype(jnp.float32).astype(jnp.bfloat16)
        earlier = dot(named.astype(jnp.bfloat16), order, ((1,), (0,)))
        rank_ref[...] = jnp.where(named > 0.5, earlier, -1.0)
        droute_ref[...] = jnp.zeros_like(droute_ref)

    slots = lax.broadcasted_iota(jnp.int32, (rows, total), 0).astype(jnp.float32)
    chosen = rank_ref[pl.ds(expert, 1), :] == slots
    pick = chosen.astype(jnp.float32).astype(jnp.bfloat16)
    start = pl.multiple_of(expert * rows, rows)
    pick_ref[pl.ds(start, rows), :] = pick
    scale_w = jnp.sum(
        jnp.where(chosen, dense_ref[pl.ds(expert, 1), :], 0.0), axis=1, keepdims=True
    )
    x = jnp.concatenate(
        [dot(pick, x_ref[h], ((1,), (0,))).astype(jnp.bfloat16) for h in range(heads)], axis=1
    )
    dy = jnp.concatenate(
        [dot(pick, dy_ref[h], ((1,), (0,))).astype(jnp.bfloat16) for h in range(heads)], axis=1
    )
    w_both = jnp.concatenate([wg_ref[0], wu_ref[0]], axis=1)
    pre = dot(x, w_both, ((1,), (0,)))
    gate_pre = pre[:, :hidden]
    up_pre = pre[:, hidden:]
    back_proj = dot(dy, wd_ref[0], ((1,), (1,)))
    sigmoid_gate = jax.nn.sigmoid(gate_pre)
    silu_gate = gate_pre * sigmoid_gate
    active = silu_gate * up_pre
    route_part = jnp.sum(active * back_proj, axis=1, keepdims=True)
    route_row = jnp.sum(jnp.where(chosen, route_part, 0.0), axis=0, keepdims=True)
    droute_ref[...] += jnp.where(routes_ref[...] == expert, route_row, 0.0)
    d_active = scale_w * back_proj
    d_gate = d_active * up_pre * sigmoid_gate * (1.0 + gate_pre * (1.0 - sigmoid_gate))
    d_up = d_active * silu_gate
    d_both = jnp.concatenate([d_gate, d_up], axis=1).astype(jnp.bfloat16)
    weighted = (scale_w * active).astype(jnp.bfloat16)
    back_ref[pl.ds(start, rows), :] = dot(d_both, w_both, ((1,), (1,))).astype(jnp.bfloat16)
    grad_both = dot(x, d_both, ((0,), (0,))).astype(jnp.bfloat16)
    gg_ref[0] = grad_both[:, :hidden]
    gu_ref[0] = grad_both[:, hidden:]
    gd_ref[0] = dot(weighted, dy, ((0,), (0,))).astype(jnp.bfloat16)

    @pl.when(expert == experts - 1)
    def _():
        for h in range(heads):
            dmoe_ref[h] = dot(
                pick_ref[...], back_ref[:, h * quarter : (h + 1) * quarter], ((0,), (0,))
            ).astype(jnp.bfloat16)


def run_experts(routes_t, weight_t, x, dy, w_gate, w_up, w_down):
    local, width, hidden = w_gate.shape
    heads, total, quarter = x.shape
    shard_count = lax.axis_size("seq")
    rows = -(-shard_count * CAP // 16) * 16
    whole = lambda *shape: pl.BlockSpec(shape, lambda e: (0,) * len(shape))
    wide = pl.BlockSpec((1, width, hidden), lambda e: (e, 0, 0))
    tall = pl.BlockSpec((1, hidden, width), lambda e: (e, 0, 0))
    return pl.pallas_call(
        expert_kernel,
        grid=(local,),
        in_specs=[
            whole(*routes_t.shape),
            whole(*weight_t.shape),
            whole(*x.shape),
            whole(*dy.shape),
            wide,
            wide,
            tall,
        ],
        out_specs=[wide, wide, tall, whole(*x.shape), whole(*weight_t.shape)],
        out_shape=[
            jax.ShapeDtypeStruct(w_gate.shape, jnp.bfloat16),
            jax.ShapeDtypeStruct(w_up.shape, jnp.bfloat16),
            jax.ShapeDtypeStruct(w_down.shape, jnp.bfloat16),
            jax.ShapeDtypeStruct(x.shape, jnp.bfloat16),
            jax.ShapeDtypeStruct(weight_t.shape, jnp.float32),
        ],
        scratch_shapes=[
            pltpu.VMEM((local, total), jnp.float32),
            pltpu.VMEM((local, total), jnp.float32),
            pltpu.VMEM((local * rows, total), jnp.bfloat16),
            pltpu.VMEM((local * rows, width), jnp.bfloat16),
        ],
        compiler_params=pltpu.CompilerParams(vmem_limit_bytes=60 << 20),
        name="experts",
    )(routes_t, weight_t, x, dy, w_gate, w_up, w_down)


def gathered_experts(moe_in, grad_out, routes, route_weight, w_gate, w_up, w_down):
    local = w_gate.shape[0]
    both = jnp.stack([moe_in, grad_out])
    by_seq = lax.all_gather(both, "seq", axis=1, tiled=True)
    x, dy = jnp.moveaxis(lax.all_gather(by_seq, "head", axis=0), 0, 1)
    tables = jnp.concatenate(
        [routes.astype(jnp.float32).T, route_weight.astype(jnp.float32).T], axis=0
    )
    tables = lax.all_gather(tables, "seq", axis=1, tiled=True)
    top = routes.shape[1]
    routes_t = tables[:top].astype(jnp.int32) - lax.axis_index("seq") * local
    grad_gate, grad_up, grad_down, d_moe, d_route = run_experts(
        routes_t, tables[top:], x, dy, w_gate, w_up, w_down
    )
    by_head = lax.psum_scatter(d_moe, "head", scatter_dimension=0, tiled=True)
    d_moe_in = lax.psum_scatter(by_head, "seq", scatter_dimension=1, tiled=True)[0]
    d_route = lax.psum(d_route, "head")
    d_route = lax.psum_scatter(d_route, "seq", scatter_dimension=1, tiled=True)
    d_route_weight = d_route.T.astype(jnp.bfloat16)
    return (d_moe_in, d_route_weight, grad_gate, grad_up, grad_down)


def shards(moe_in, grad_out, routes, route_weight, w_gate, w_up, w_down, queries, key_value):
    gathered_rows = lax.axis_size("seq") * moe_in.shape[0]
    experts = gathered_experts if gathered_rows <= EXPERTS * CAP else dispatched_experts
    d_moe_in, d_route_weight, grad_gate, grad_up, grad_down = experts(
        moe_in, grad_out, routes, route_weight, w_gate, w_up, w_down
    )
    d_queries, d_key_value = attention(grad_out, d_moe_in, queries, key_value)
    return (d_moe_in, d_route_weight, grad_gate, grad_up, grad_down, d_queries, d_key_value)


def solution(mesh):
    in_specs = (
        P(("rep", "seq"), "head"),
        P(("rep", "seq"), "head"),
        P(("rep", "seq"), None),
        P(("rep", "seq"), None),
        P("seq", None, "head"),
        P("seq", None, "head"),
        P("seq", "head", None),
        P(("rep", "seq"), "head"),
        P(("rep", "seq"), "head", None),
    )
    out_specs = (
        P(("rep", "seq"), "head"),
        P(("rep", "seq"), None),
        P(("rep", "seq"), None, "head"),
        P(("rep", "seq"), None, "head"),
        P(("rep", "seq"), "head", None),
        P(("rep", "seq"), "head"),
        P(("rep", "seq"), "head", None),
    )
    return jax.shard_map(shards, mesh=mesh, in_specs=in_specs, out_specs=out_specs, check_vma=False)
```

```python
import jax
import jax.numpy as jnp
from jax import lax
from jax.experimental import pallas as pl
from jax.experimental.pallas import tpu as pltpu
from jax.sharding import PartitionSpec as P

EXPERTS = 64
WIN = 512
CAP = 18
MESH = pl.DeviceIdType.MESH


def shifted(block, axis, distance):
    devices = range(lax.axis_size(axis))
    route = [(i - distance, i) for i in devices if i - distance in devices]
    return lax.ppermute(block, axis, route)


def slot_tables(routes, route_weight):
    token_rows, top_count = routes.shape
    flat_expert = routes.reshape(token_rows * top_count)
    expert_ids = jnp.arange(EXPERTS, dtype=jnp.int32)
    one_hot = (flat_expert[:, None] == expert_ids[None, :]).astype(jnp.int32)
    earlier = jnp.cumsum(one_hot, axis=0) - one_hot
    slot_rank = jnp.sum(earlier * one_hot, axis=1)
    target = flat_expert * CAP + slot_rank
    slot_cells = jnp.arange(EXPERTS * CAP, dtype=jnp.int32)
    chosen = (target[None, :] == slot_cells[:, None]).astype(jnp.float32)
    by_token = jnp.sum(chosen.reshape(EXPERTS * CAP, token_rows, top_count), axis=2).astype(
        jnp.bfloat16
    )
    slot_weight = jnp.dot(
        chosen,
        route_weight.reshape(token_rows * top_count).astype(jnp.float32),
        precision=lax.Precision.HIGHEST,
    )
    return (chosen, by_token, slot_weight.astype(jnp.bfloat16).reshape(EXPERTS, CAP))


def place_rows(by_token, source):
    placed = jnp.dot(by_token, source, preferred_element_type=jnp.float32)
    return placed.astype(jnp.bfloat16).reshape(EXPERTS, CAP, source.shape[1])


def fetch_window(own_rows, reach):
    earlier_shards = [shifted(own_rows, "seq", offset) for offset in range(reach, 0, -1)]
    window = jnp.concatenate(earlier_shards + [own_rows], axis=0)
    return window


def return_window(d_window, reach, shard):
    summed = d_window[reach * shard :]
    for offset in range(1, reach + 1):
        begin = (reach - offset) * shard
        summed = summed + shifted(
            d_window[begin : begin + shard].astype(jnp.bfloat16), "seq", -offset
        ).astype(jnp.float32)
    return summed


def dispatched_experts(moe_in, grad_out, routes, route_weight, w_gate, w_up, w_down):
    seq_count = lax.axis_size("seq")
    local_experts = w_gate.shape[0]
    chosen, by_token, slot_weight = slot_tables(routes, route_weight)
    part_in, part_grad, got_weight = (
        lax.all_to_all(
            place_rows(by_token, moe_in), "seq", split_axis=0, concat_axis=0, tiled=True
        ),
        lax.all_to_all(
            place_rows(by_token, grad_out), "seq", split_axis=0, concat_axis=0, tiled=True
        ),
        lax.all_to_all(slot_weight, "seq", split_axis=0, concat_axis=0, tiled=True),
    )
    got_in, got_grad = (
        lax.all_gather(part_in, "head", axis=2, tiled=True),
        lax.all_gather(part_grad, "head", axis=2, tiled=True),
    )
    width = got_in.shape[2]
    rows_in = got_in.reshape(seq_count, local_experts, CAP, width)
    rows_grad = got_grad.reshape(seq_count, local_experts, CAP, width)
    scale_w = got_weight.reshape(seq_count, local_experts, CAP).astype(jnp.float32)[..., None]
    gate_pre = jnp.einsum("secd,edf->secf", rows_in, w_gate, preferred_element_type=jnp.float32)
    up_pre = jnp.einsum("secd,edf->secf", rows_in, w_up, preferred_element_type=jnp.float32)
    back_proj = jnp.einsum("secd,efd->secf", rows_grad, w_down, preferred_element_type=jnp.float32)
    sigmoid_gate = jax.nn.sigmoid(gate_pre)
    silu_gate = gate_pre * sigmoid_gate
    active = silu_gate * up_pre
    route_part = jnp.sum(active * back_proj, axis=3)
    d_active = scale_w * back_proj
    d_gate = (d_active * up_pre * sigmoid_gate * (1.0 + gate_pre * (1.0 - sigmoid_gate))).astype(
        jnp.bfloat16
    )
    d_up = (d_active * silu_gate).astype(jnp.bfloat16)
    weighted = (scale_w * active).astype(jnp.bfloat16)
    rows_back = jnp.einsum("secf,edf->secd", d_gate, w_gate, preferred_element_type=jnp.float32)
    rows_back = rows_back + jnp.einsum(
        "secf,edf->secd", d_up, w_up, preferred_element_type=jnp.float32
    )
    rows_quarter = lax.psum_scatter(
        rows_back.reshape(seq_count * local_experts, CAP, width).astype(jnp.bfloat16),
        "head",
        scatter_dimension=2,
        tiled=True,
    )
    route_sum = lax.psum(route_part, "head").astype(jnp.bfloat16)
    grad_gate = jnp.einsum(
        "secd,secf->edf", rows_in, d_gate, preferred_element_type=jnp.float32
    ).astype(jnp.bfloat16)
    grad_up = jnp.einsum(
        "secd,secf->edf", rows_in, d_up, preferred_element_type=jnp.float32
    ).astype(jnp.bfloat16)
    grad_down = jnp.einsum(
        "secf,secd->efd", weighted, rows_grad, preferred_element_type=jnp.float32
    ).astype(jnp.bfloat16)
    back_rows, back_weight = (
        lax.all_to_all(rows_quarter, "seq", split_axis=0, concat_axis=0, tiled=True),
        lax.all_to_all(
            route_sum.reshape(seq_count * local_experts, CAP),
            "seq",
            split_axis=0,
            concat_axis=0,
            tiled=True,
        ),
    )
    quarter = back_rows.shape[2]
    d_moe_in = jnp.einsum(
        "st,sd->td",
        by_token,
        back_rows.reshape(EXPERTS * CAP, quarter),
        preferred_element_type=jnp.float32,
    ).astype(jnp.bfloat16)
    d_route = jnp.dot(
        back_weight.reshape(EXPERTS * CAP).astype(jnp.float32),
        chosen,
        precision=lax.Precision.HIGHEST,
    )
    d_route_weight = d_route.astype(jnp.bfloat16).reshape(routes.shape)
    return (d_moe_in, d_route_weight, grad_gate, grad_up, grad_down)


def attend(grad_out, d_moe_in, queries, window, first_shard):
    tokens = grad_out.shape[0]
    head_dim = window.shape[1] // 2
    per_group = queries.shape[1] // head_dim
    scale = head_dim ** (-0.5)
    d_hidden = (grad_out.astype(jnp.float32) + d_moe_in.astype(jnp.float32)).astype(jnp.bfloat16)
    query_rows = queries.reshape(tokens * per_group, head_dim)
    grad_rows = d_hidden.reshape(tokens * per_group, head_dim)
    key_rows = window[:, :head_dim]
    value_rows = window[:, head_dim:]
    contract_last = (((1,), (1,)), ((), ()))
    contract_first = (((0,), (0,)), ((), ()))
    seq_index = lax.axis_index("seq")
    key_pos = first_shard * tokens + jnp.arange(window.shape[0], dtype=jnp.int32)
    row_total = tokens * per_group
    block_rows = min(512, row_total)
    block_count = row_total // block_rows

    def attend_block(index, carry):
        d_window, d_query_all = carry
        begin = (index * block_rows).astype(jnp.int32)
        query_blk = lax.dynamic_slice_in_dim(query_rows, begin, block_rows, 0)
        grad_blk = lax.dynamic_slice_in_dim(grad_rows, begin, block_rows, 0)
        scores = (
            lax.dot_general(query_blk, key_rows, contract_last, preferred_element_type=jnp.float32)
            * scale
        )
        position = (
            seq_index * tokens + (begin + jnp.arange(block_rows, dtype=jnp.int32)) // per_group
        )
        visible = (
            (key_pos[None, :] >= 0)
            & (key_pos[None, :] <= position[:, None])
            & (key_pos[None, :] > position[:, None] - WIN)
        )
        scores = jnp.where(visible, scores, -1e30)
        row_max = jnp.max(scores, axis=1, keepdims=True)
        raised = jnp.exp(scores - row_max)
        probs = raised / jnp.sum(raised, axis=1, keepdims=True)
        d_probs = lax.dot_general(
            grad_blk, value_rows, contract_last, preferred_element_type=jnp.float32
        )
        row_dot = jnp.sum(probs * d_probs, axis=1, keepdims=True)
        d_scores = (probs * (d_probs - row_dot) * scale).astype(jnp.bfloat16)
        probs_low = probs.astype(jnp.bfloat16)
        d_query_blk = jnp.dot(d_scores, key_rows, preferred_element_type=jnp.float32).astype(
            jnp.bfloat16
        )
        d_keys = lax.dot_general(
            d_scores, query_blk, contract_first, preferred_element_type=jnp.float32
        )
        d_values = lax.dot_general(
            probs_low, grad_blk, contract_first, preferred_element_type=jnp.float32
        )
        d_window = d_window + jnp.concatenate([d_keys, d_values], axis=1)
        d_query_all = lax.dynamic_update_slice_in_dim(d_query_all, d_query_blk, begin, 0)
        return (d_window, d_query_all)

    window_start = jnp.zeros(window.shape, jnp.float32)
    query_start = jnp.zeros((row_total, head_dim), jnp.bfloat16)
    d_window, d_query_all = lax.fori_loop(0, block_count, attend_block, (window_start, query_start))
    d_queries = d_query_all.reshape(tokens, per_group * head_dim)
    return (d_queries, d_window)


def attention(grad_out, d_moe_in, queries, key_value):
    tokens = grad_out.shape[0]
    reach = min(WIN // tokens, lax.axis_size("seq") - 1)
    window = fetch_window(key_value.reshape(tokens, key_value.shape[2]), reach)
    first_shard = lax.axis_index("seq") - reach
    d_queries, d_window = attend(grad_out, d_moe_in, queries, window, first_shard)
    d_own = return_window(d_window, reach, tokens)
    d_key_value = d_own.astype(jnp.bfloat16).reshape(key_value.shape)
    return (d_queries, d_key_value)


def dot(a, b, contract):
    return lax.dot_general(a, b, (contract, ((), ())), preferred_element_type=jnp.float32)


def expert_kernel(
    tables_ref,
    tokens_ref,
    wg_ref,
    wu_ref,
    wd_ref,
    gg_ref,
    gu_ref,
    gd_ref,
    dmoe_ref,
    routes_ref,
    weight_ref,
    droute_ref,
    rank_ref,
    dense_ref,
    pick_ref,
    back_ref,
):
    expert = pl.program_id(0)
    experts = pl.num_programs(0)
    _, heads, total, quarter = tokens_ref.shape
    shard_count, double_top, shard = tables_ref.shape
    top = double_top // 2
    hidden = wg_ref.shape[2]
    rows = pick_ref.shape[0] // rank_ref.shape[0]
    local = rank_ref.shape[0]

    @pl.when(expert == 0)
    def _():
        first = (lax.axis_index("seq") * local).astype(jnp.float32)
        for s in range(shard_count):
            columns = slice(s * shard, (s + 1) * shard)
            routes_ref[:, columns] = tables_ref[s, :top, :] - first
            weight_ref[:, columns] = tables_ref[s, top:, :]
        for index in range(local):
            hit = routes_ref[...] == index
            named = jnp.sum(hit.astype(jnp.float32), axis=0, keepdims=True)
            rank_ref[pl.ds(index, 1), :] = named
            dense_ref[pl.ds(index, 1), :] = jnp.sum(
                jnp.where(hit, weight_ref[...], 0.0), axis=0, keepdims=True
            )
        named = rank_ref[...]
        before = lax.broadcasted_iota(jnp.int32, (total, total), 0)
        after = lax.broadcasted_iota(jnp.int32, (total, total), 1)
        order = (before < after).astype(jnp.float32).astype(jnp.bfloat16)
        earlier = dot(named.astype(jnp.bfloat16), order, ((1,), (0,)))
        rank_ref[...] = jnp.where(named > 0.5, earlier, -1.0)
        droute_ref[...] = jnp.zeros_like(droute_ref)

    slots = lax.broadcasted_iota(jnp.int32, (rows, total), 0).astype(jnp.float32)
    chosen = rank_ref[pl.ds(expert, 1), :] == slots
    pick = chosen.astype(jnp.float32).astype(jnp.bfloat16)
    start = pl.multiple_of(expert * rows, rows)
    pick_ref[pl.ds(start, rows), :] = pick
    scale_w = jnp.sum(
        jnp.where(chosen, dense_ref[pl.ds(expert, 1), :], 0.0), axis=1, keepdims=True
    )
    x = jnp.concatenate(
        [dot(pick, tokens_ref[0, h], ((1,), (0,))).astype(jnp.bfloat16) for h in range(heads)], axis=1
    )
    dy = jnp.concatenate(
        [dot(pick, tokens_ref[1, h], ((1,), (0,))).astype(jnp.bfloat16) for h in range(heads)], axis=1
    )
    w_both = jnp.concatenate([wg_ref[0], wu_ref[0]], axis=1)
    pre = dot(x, w_both, ((1,), (0,)))
    gate_pre = pre[:, :hidden]
    up_pre = pre[:, hidden:]
    back_proj = dot(dy, wd_ref[0], ((1,), (1,)))
    sigmoid_gate = jax.nn.sigmoid(gate_pre)
    silu_gate = gate_pre * sigmoid_gate
    active = silu_gate * up_pre
    route_part = jnp.sum(active * back_proj, axis=1, keepdims=True)
    route_row = jnp.sum(jnp.where(chosen, route_part, 0.0), axis=0, keepdims=True)
    droute_ref[...] += jnp.where(routes_ref[...] == expert.astype(jnp.float32), route_row, 0.0)
    d_active = scale_w * back_proj
    d_gate = d_active * up_pre * sigmoid_gate * (1.0 + gate_pre * (1.0 - sigmoid_gate))
    d_up = d_active * silu_gate
    d_both = jnp.concatenate([d_gate, d_up], axis=1).astype(jnp.bfloat16)
    weighted = (scale_w * active).astype(jnp.bfloat16)
    back_ref[pl.ds(start, rows), :] = dot(d_both, w_both, ((1,), (1,))).astype(jnp.bfloat16)
    grad_both = dot(x, d_both, ((0,), (0,))).astype(jnp.bfloat16)
    gg_ref[0] = grad_both[:, :hidden]
    gu_ref[0] = grad_both[:, hidden:]
    gd_ref[0] = dot(weighted, dy, ((0,), (0,))).astype(jnp.bfloat16)

    @pl.when(expert == experts - 1)
    def _():
        for h in range(heads):
            columns = slice(h * quarter, (h + 1) * quarter)
            summed = dot(pick_ref[...], back_ref[:, columns], ((0,), (0,))).astype(jnp.bfloat16)
            for s in range(shard_count):
                dmoe_ref[h, s, :shard, :] = summed[s * shard : (s + 1) * shard]
                share = droute_ref[:, s * shard : (s + 1) * shard]
                share = jnp.concatenate([share, jnp.zeros((16 - top, shard), jnp.float32)], axis=0)
                if quarter > shard:
                    blank = jnp.zeros((16, quarter - shard), jnp.float32)
                    share = jnp.concatenate([share, blank], axis=1)
                dmoe_ref[h, s, shard:, :] = share.astype(jnp.bfloat16)


def run_experts(tables, tokens, w_gate, w_up, w_down):
    local, width, hidden = w_gate.shape
    _, heads, total, quarter = tokens.shape
    shard_count, double_top, shard = tables.shape
    top = double_top // 2
    rows = -(-shard_count * CAP // 16) * 16
    whole = lambda *shape: pl.BlockSpec(shape, lambda e: (0,) * len(shape))
    wide = pl.BlockSpec((1, width, hidden), lambda e: (e, 0, 0))
    tall = pl.BlockSpec((1, hidden, width), lambda e: (e, 0, 0))
    back_shape = (heads, shard_count, shard + 16, quarter)
    return pl.pallas_call(
        expert_kernel,
        grid=(local,),
        in_specs=[whole(*tables.shape), whole(*tokens.shape), wide, wide, tall],
        out_specs=[wide, wide, tall, whole(*back_shape)],
        out_shape=[
            jax.ShapeDtypeStruct(w_gate.shape, jnp.bfloat16),
            jax.ShapeDtypeStruct(w_up.shape, jnp.bfloat16),
            jax.ShapeDtypeStruct(w_down.shape, jnp.bfloat16),
            jax.ShapeDtypeStruct(back_shape, jnp.bfloat16),
        ],
        scratch_shapes=[
            pltpu.VMEM((top, total), jnp.float32),
            pltpu.VMEM((top, total), jnp.float32),
            pltpu.VMEM((top, total), jnp.float32),
            pltpu.VMEM((local, total), jnp.float32),
            pltpu.VMEM((local, total), jnp.float32),
            pltpu.VMEM((local * rows, total), jnp.bfloat16),
            pltpu.VMEM((local * rows, width), jnp.bfloat16),
        ],
        compiler_params=pltpu.CompilerParams(vmem_limit_bytes=60 << 20),
        name="experts",
    )(tables, tokens, w_gate, w_up, w_down)


def head_neighbours():
    head = lax.axis_index("head")
    return head, head + 1 - 2 * (head % 2), (head + 2) % 4, (head + 3 - 2 * (head % 2)) % 4


def inside(index, count):
    return (index >= 0) & (index < count)


def greet(along, across):
    seq = lax.axis_index("seq")
    count = lax.axis_size("seq")
    barrier = pltpu.get_barrier_semaphore()
    for peer in across:
        pl.semaphore_signal(barrier, inc=1, device_id={"head": peer}, device_id_type=MESH)
    for step in along:

        @pl.when(inside(seq + step, count))
        def _():
            pl.semaphore_signal(
                barrier, inc=1, device_id={"seq": seq + step}, device_id_type=MESH
            )

    ends = (seq == 0).astype(jnp.int32) + (seq == count - 1).astype(jnp.int32)
    pl.semaphore_wait(barrier, len(across) + len(along) - ends)


def send(source, target, send_sem, recv_sem, peer):
    return pltpu.make_async_remote_copy(
        src_ref=source,
        dst_ref=target,
        send_sem=send_sem,
        recv_sem=recv_sem,
        device_id=peer,
        device_id_type=MESH,
    )


def gather_kernel(
    in_ref,
    grad_ref,
    table_ref,
    kv_ref,
    tokens_ref,
    tables_ref,
    window_ref,
    own_sem,
    line_send,
    line_recv,
    square_send,
    square_recv,
):
    seq = lax.axis_index("seq")
    count = lax.axis_size("seq")
    shard = in_ref.shape[0]
    half = shard // 2
    head, beside, above, corner = head_neighbours()

    def piece(of, p):
        return tokens_ref.at[:, of, pl.ds(p * shard, shard), :]

    def upper(of, p):
        return tokens_ref.at[:, of, pl.ds(p * shard, half), :]

    def lower(of, p):
        return tokens_ref.at[:, of, pl.ds(p * shard + half, half), :]

    own_rows = pl.ds(seq * shard, shard)
    own = [
        pltpu.make_async_copy(in_ref, tokens_ref.at[0, head, own_rows, :], own_sem.at[0]),
        pltpu.make_async_copy(grad_ref, tokens_ref.at[1, head, own_rows, :], own_sem.at[1]),
        pltpu.make_async_copy(table_ref, tables_ref.at[seq], own_sem.at[2]),
        pltpu.make_async_copy(kv_ref, window_ref.at[seq], own_sem.at[3]),
    ]
    for copy in own:
        copy.start()
    greet((-1, 1), (beside, above))
    for copy in own:
        copy.wait()

    def line(way, p, to):
        refs = (piece(head, p), tables_ref.at[p], window_ref.at[p])
        return [
            send(ref, ref, line_send.at[way, j, p], line_recv.at[way, j, p], {"seq": to})
            for j, ref in enumerate(refs)
        ]

    def square(kind, ref, p, to):
        return send(ref, ref, square_send.at[kind, p], square_recv.at[kind, p], {"head": to})

    def forward(p):
        square(0, piece(beside, p), p, beside).wait_recv()
        square(2, upper(beside, p), p, above).start()
        square(1, piece(above, p), p, above).wait_recv()
        square(3, lower(above, p), p, beside).start()

    ways = ((0, 1), (1, -1))
    for k in range(count):
        for way, step in ways:
            p = seq - step * k

            @pl.when(inside(p, count))
            def _():
                if k > 0:
                    for copy in line(way, p, seq - step):
                        copy.wait_recv()

                @pl.when(inside(seq + step, count))
                def _():
                    for copy in line(way, p, seq + step):
                        copy.start()

                if k > 0 or way == 0:
                    square(0, piece(head, p), p, beside).start()
                    square(1, piece(head, p), p, above).start()

        if k > 0:
            for way, step in ways:
                if k > 1 or way == 0:
                    p = seq - step * (k - 1)
                    pl.when(inside(p, count))(lambda p=p: forward(p))
    for way, step in ways:
        if count > 1 or way == 0:
            p = seq - step * (count - 1)
            pl.when(inside(p, count))(lambda p=p: forward(p))
    for p in range(count):
        square(2, upper(corner, p), p, above).wait_recv()
        square(3, lower(corner, p), p, beside).wait_recv()
        square(0, piece(head, p), p, beside).wait_send()
        square(1, piece(head, p), p, above).wait_send()
        square(2, upper(beside, p), p, above).wait_send()
        square(3, lower(above, p), p, beside).wait_send()
    for k in range(count):
        for way, step in ways:
            p = seq - step * k

            @pl.when(inside(p, count) & inside(seq + step, count))
            def _():
                for copy in line(way, p, seq + step):
                    copy.wait_send()


def gather_tokens(moe_in, grad_out, table, key_value):
    heads = lax.axis_size("head")
    count = lax.axis_size("seq")
    shard, quarter = moe_in.shape
    return pl.pallas_call(
        gather_kernel,
        in_specs=[pl.BlockSpec(memory_space=pltpu.VMEM)] * 4,
        out_specs=[pl.BlockSpec(memory_space=pltpu.VMEM)] * 3,
        out_shape=[
            jax.ShapeDtypeStruct((2, heads, count * shard, quarter), jnp.bfloat16),
            jax.ShapeDtypeStruct((count,) + table.shape, jnp.float32),
            jax.ShapeDtypeStruct((count,) + key_value.shape, jnp.bfloat16),
        ],
        scratch_shapes=[
            pltpu.SemaphoreType.DMA((4,)),
            pltpu.SemaphoreType.DMA((2, 3, count)),
            pltpu.SemaphoreType.DMA((2, 3, count)),
            pltpu.SemaphoreType.DMA((4, count)),
            pltpu.SemaphoreType.DMA((4, count)),
        ],
        compiler_params=pltpu.CompilerParams(collective_id=0, has_side_effects=True),
        name="gather_tokens",
    )(moe_in, grad_out, table, key_value)


def reduce_kernel(
    part_ref,
    total_ref,
    beside_half,
    above_half,
    beside_full,
    above_full,
    to_beside,
    to_above,
    to_line,
    from_line,
    send_sem,
    recv_sem,
):
    seq = lax.axis_index("seq")
    count = lax.axis_size("seq")
    half = beside_half.shape[1]
    head, beside, above, corner = head_neighbours()
    greet((-1, 1), (beside, above))

    def pair(kind, source, target, p, peer):
        return send(source, target, send_sem.at[kind, p], recv_sem.at[kind, p], peer)

    def first(p):
        return (
            pair(
                0,
                part_ref.at[corner, p, pl.ds(0, half), :],
                beside_half.at[p],
                p,
                {"head": beside},
            ),
            pair(
                1,
                part_ref.at[corner, p, pl.ds(half, part_ref.shape[2] - half), :],
                above_half.at[p],
                p,
                {"head": above},
            ),
        )

    def second(p):
        return (
            pair(2, to_beside.at[p], beside_full.at[p], p, {"head": beside}),
            pair(3, to_above.at[p], above_full.at[p], p, {"head": above}),
        )

    def line(way, p, to):
        return pair(4 + way, to_line.at[p], from_line.at[way, p], p, {"seq": to})

    def each(body):
        for k in reversed(range(count)):
            for way, step in ((0, 1), (1, -1)):
                if k > 0 or way == 0:
                    p = seq + step * k
                    pl.when(inside(p, count))(lambda k=k, way=way, step=step, p=p: body(k, way, step, p))

    def start_first(k, way, step, p):
        for copy in first(p):
            copy.start()

    def add_first(k, way, step, p):
        from_beside, from_above = first(p)
        via_beside, via_above = second(p)
        from_beside.wait_recv()
        to_above[p, :half, :] = (
            part_ref[above, p, :half, :].astype(jnp.float32)
            + beside_half[p].astype(jnp.float32)
        ).astype(jnp.bfloat16)
        to_above[p, half:, :] = part_ref[above, p, half:, :]
        via_above.start()
        from_above.wait_recv()
        to_beside[p, :half, :] = part_ref[beside, p, :half, :]
        to_beside[p, half:, :] = (
            part_ref[beside, p, half:, :].astype(jnp.float32) + above_half[p].astype(jnp.float32)
        ).astype(jnp.bfloat16)
        via_beside.start()

    def add_second(k, way, step, p):
        for copy in second(p):
            copy.wait_recv()
        summed = (
            part_ref[head, p].astype(jnp.float32)
            + beside_full[p].astype(jnp.float32)
            + above_full[p].astype(jnp.float32)
        )
        if k > 0:
            to_line[p] = summed.astype(jnp.bfloat16)

            @pl.when(inside(seq - step, count))
            def _():
                line(way, p, seq - step).wait_recv()
                to_line[p] = (summed + from_line[way, p].astype(jnp.float32)).astype(jnp.bfloat16)

            line(way, p, seq + step).start()
        else:
            for other in range(count):

                @pl.when(seq == other)
                def _():
                    result = summed
                    if other > 0:
                        line(0, p, seq - 1).wait_recv()
                        result = result + from_line[0, p].astype(jnp.float32)
                    if other < count - 1:
                        line(1, p, seq + 1).wait_recv()
                        result = result + from_line[1, p].astype(jnp.float32)
                    total_ref[...] = result.astype(jnp.bfloat16)

    def finish(k, way, step, p):
        for copy in first(p) + second(p):
            copy.wait_send()
        if k > 0:
            line(way, p, seq + step).wait_send()

    each(start_first)
    each(add_first)
    each(add_second)
    each(finish)


def reduce_tokens(part):
    _, count, rows, quarter = part.shape
    half = (rows - 16) // 2
    block = lambda *lead: pltpu.VMEM(lead + (rows, quarter), jnp.bfloat16)
    return pl.pallas_call(
        reduce_kernel,
        in_specs=[pl.BlockSpec(memory_space=pltpu.VMEM)],
        out_specs=pl.BlockSpec(memory_space=pltpu.VMEM),
        out_shape=jax.ShapeDtypeStruct((rows, quarter), jnp.bfloat16),
        scratch_shapes=[
            pltpu.VMEM((count, half, quarter), jnp.bfloat16),
            pltpu.VMEM((count, rows - half, quarter), jnp.bfloat16),
            block(count),
            block(count),
            block(count),
            block(count),
            block(count),
            block(2, count),
            pltpu.SemaphoreType.DMA((6, count)),
            pltpu.SemaphoreType.DMA((6, count)),
        ],
        compiler_params=pltpu.CompilerParams(collective_id=1, has_side_effects=True),
        name="reduce_tokens",
    )(part)


def return_kernel(part_ref, total_ref, landed, send_sem, recv_sem):
    seq = lax.axis_index("seq")
    count = lax.axis_size("seq")
    barrier = pltpu.get_barrier_semaphore()
    for offset in range(1, count):
        pl.semaphore_signal(
            barrier, inc=1, device_id={"seq": (seq + offset) % count}, device_id_type=MESH
        )
    pl.semaphore_wait(barrier, count - 1)
    copies = []
    for offset in range(1, count):
        to = (seq + offset) % count
        copies.append(
            send(
                part_ref.at[to],
                landed.at[offset],
                send_sem.at[offset],
                recv_sem.at[offset],
                {"seq": to},
            )
        )
        copies[-1].start()
    summed = part_ref[seq].astype(jnp.float32)
    for offset, copy in enumerate(copies, 1):
        copy.wait_recv()
        summed = summed + landed[offset].astype(jnp.float32)
    total_ref[...] = summed.astype(jnp.bfloat16)
    for copy in copies:
        copy.wait_send()


def return_shards(part):
    count, shard, width = part.shape
    return pl.pallas_call(
        return_kernel,
        in_specs=[pl.BlockSpec(memory_space=pltpu.VMEM)],
        out_specs=pl.BlockSpec(memory_space=pltpu.VMEM),
        out_shape=jax.ShapeDtypeStruct((shard, width), jnp.bfloat16),
        scratch_shapes=[
            pltpu.VMEM(part.shape, jnp.bfloat16),
            pltpu.SemaphoreType.DMA((count,)),
            pltpu.SemaphoreType.DMA((count,)),
        ],
        compiler_params=pltpu.CompilerParams(collective_id=2, has_side_effects=True),
        name="return_shards",
    )(part)


def gathered_layer(moe_in, grad_out, routes, route_weight, w_gate, w_up, w_down, queries, key_value):
    shard, top = routes.shape
    table = jnp.concatenate(
        [routes.astype(jnp.float32).T, route_weight.astype(jnp.float32).T], axis=0
    )
    own_rows = key_value.reshape(shard, key_value.shape[2])
    tokens, tables, window = gather_tokens(moe_in, grad_out, table, own_rows)
    grad_gate, grad_up, grad_down, d_moe = run_experts(tables, tokens, w_gate, w_up, w_down)
    summed = reduce_tokens(d_moe)
    d_moe_in = summed[:shard]
    d_route_weight = summed[shard : shard + top, :shard].T
    d_queries, d_window = attend(
        grad_out, d_moe_in, queries, window.reshape(-1, window.shape[2]), 0
    )
    d_own = return_shards(d_window.astype(jnp.bfloat16).reshape(window.shape))
    d_key_value = d_own.reshape(key_value.shape)
    return (d_moe_in, d_route_weight, grad_gate, grad_up, grad_down, d_queries, d_key_value)


def shards(moe_in, grad_out, routes, route_weight, w_gate, w_up, w_down, queries, key_value):
    gathered_rows = lax.axis_size("seq") * moe_in.shape[0]
    if gathered_rows <= EXPERTS * CAP and lax.axis_size("head") == 4:
        return gathered_layer(
            moe_in, grad_out, routes, route_weight, w_gate, w_up, w_down, queries, key_value
        )
    d_moe_in, d_route_weight, grad_gate, grad_up, grad_down = dispatched_experts(
        moe_in, grad_out, routes, route_weight, w_gate, w_up, w_down
    )
    d_queries, d_key_value = attention(grad_out, d_moe_in, queries, key_value)
    return (d_moe_in, d_route_weight, grad_gate, grad_up, grad_down, d_queries, d_key_value)


def solution(mesh):
    in_specs = (
        P(("rep", "seq"), "head"),
        P(("rep", "seq"), "head"),
        P(("rep", "seq"), None),
        P(("rep", "seq"), None),
        P("seq", None, "head"),
        P("seq", None, "head"),
        P("seq", "head", None),
        P(("rep", "seq"), "head"),
        P(("rep", "seq"), "head", None),
    )
    out_specs = (
        P(("rep", "seq"), "head"),
        P(("rep", "seq"), None),
        P(("rep", "seq"), None, "head"),
        P(("rep", "seq"), None, "head"),
        P(("rep", "seq"), "head", None),
        P(("rep", "seq"), "head"),
        P(("rep", "seq"), "head", None),
    )
    return jax.shard_map(shards, mesh=mesh, in_specs=in_specs, out_specs=out_specs, check_vma=False)
```

```python
import jax
import jax.numpy as jnp
from jax import lax
from jax.experimental import pallas as pl
from jax.experimental.pallas import tpu as pltpu
from jax.sharding import PartitionSpec as P

EXPERTS = 64
WIN = 512
CAP = 18
MESH = pl.DeviceIdType.MESH


def shifted(block, axis, distance):
    devices = range(lax.axis_size(axis))
    route = [(i - distance, i) for i in devices if i - distance in devices]
    return lax.ppermute(block, axis, route)


def slot_tables(routes, route_weight):
    token_rows, top_count = routes.shape
    flat_expert = routes.reshape(token_rows * top_count)
    expert_ids = jnp.arange(EXPERTS, dtype=jnp.int32)
    one_hot = (flat_expert[:, None] == expert_ids[None, :]).astype(jnp.int32)
    earlier = jnp.cumsum(one_hot, axis=0) - one_hot
    slot_rank = jnp.sum(earlier * one_hot, axis=1)
    target = flat_expert * CAP + slot_rank
    slot_cells = jnp.arange(EXPERTS * CAP, dtype=jnp.int32)
    chosen = (target[None, :] == slot_cells[:, None]).astype(jnp.float32)
    by_token = jnp.sum(chosen.reshape(EXPERTS * CAP, token_rows, top_count), axis=2).astype(
        jnp.bfloat16
    )
    slot_weight = jnp.dot(
        chosen,
        route_weight.reshape(token_rows * top_count).astype(jnp.float32),
        precision=lax.Precision.HIGHEST,
    )
    return (chosen, by_token, slot_weight.astype(jnp.bfloat16).reshape(EXPERTS, CAP))


def place_rows(by_token, source):
    placed = jnp.dot(by_token, source, preferred_element_type=jnp.float32)
    return placed.astype(jnp.bfloat16).reshape(EXPERTS, CAP, source.shape[1])


def fetch_window(own_rows, reach):
    earlier_shards = [shifted(own_rows, "seq", offset) for offset in range(reach, 0, -1)]
    window = jnp.concatenate(earlier_shards + [own_rows], axis=0)
    return window


def return_window(d_window, reach, shard):
    summed = d_window[reach * shard :]
    for offset in range(1, reach + 1):
        begin = (reach - offset) * shard
        summed = summed + shifted(
            d_window[begin : begin + shard].astype(jnp.bfloat16), "seq", -offset
        ).astype(jnp.float32)
    return summed


def dispatched_experts(moe_in, grad_out, routes, route_weight, w_gate, w_up, w_down):
    seq_count = lax.axis_size("seq")
    local_experts = w_gate.shape[0]
    chosen, by_token, slot_weight = slot_tables(routes, route_weight)
    part_in, part_grad, got_weight = (
        lax.all_to_all(
            place_rows(by_token, moe_in), "seq", split_axis=0, concat_axis=0, tiled=True
        ),
        lax.all_to_all(
            place_rows(by_token, grad_out), "seq", split_axis=0, concat_axis=0, tiled=True
        ),
        lax.all_to_all(slot_weight, "seq", split_axis=0, concat_axis=0, tiled=True),
    )
    got_in, got_grad = (
        lax.all_gather(part_in, "head", axis=2, tiled=True),
        lax.all_gather(part_grad, "head", axis=2, tiled=True),
    )
    width = got_in.shape[2]
    rows_in = got_in.reshape(seq_count, local_experts, CAP, width)
    rows_grad = got_grad.reshape(seq_count, local_experts, CAP, width)
    scale_w = got_weight.reshape(seq_count, local_experts, CAP).astype(jnp.float32)[..., None]
    gate_pre = jnp.einsum("secd,edf->secf", rows_in, w_gate, preferred_element_type=jnp.float32)
    up_pre = jnp.einsum("secd,edf->secf", rows_in, w_up, preferred_element_type=jnp.float32)
    back_proj = jnp.einsum("secd,efd->secf", rows_grad, w_down, preferred_element_type=jnp.float32)
    sigmoid_gate = jax.nn.sigmoid(gate_pre)
    silu_gate = gate_pre * sigmoid_gate
    active = silu_gate * up_pre
    route_part = jnp.sum(active * back_proj, axis=3)
    d_active = scale_w * back_proj
    d_gate = (d_active * up_pre * sigmoid_gate * (1.0 + gate_pre * (1.0 - sigmoid_gate))).astype(
        jnp.bfloat16
    )
    d_up = (d_active * silu_gate).astype(jnp.bfloat16)
    weighted = (scale_w * active).astype(jnp.bfloat16)
    rows_back = jnp.einsum("secf,edf->secd", d_gate, w_gate, preferred_element_type=jnp.float32)
    rows_back = rows_back + jnp.einsum(
        "secf,edf->secd", d_up, w_up, preferred_element_type=jnp.float32
    )
    rows_quarter = lax.psum_scatter(
        rows_back.reshape(seq_count * local_experts, CAP, width).astype(jnp.bfloat16),
        "head",
        scatter_dimension=2,
        tiled=True,
    )
    route_sum = lax.psum(route_part, "head").astype(jnp.bfloat16)
    grad_gate = jnp.einsum(
        "secd,secf->edf", rows_in, d_gate, preferred_element_type=jnp.float32
    ).astype(jnp.bfloat16)
    grad_up = jnp.einsum(
        "secd,secf->edf", rows_in, d_up, preferred_element_type=jnp.float32
    ).astype(jnp.bfloat16)
    grad_down = jnp.einsum(
        "secf,secd->efd", weighted, rows_grad, preferred_element_type=jnp.float32
    ).astype(jnp.bfloat16)
    back_rows, back_weight = (
        lax.all_to_all(rows_quarter, "seq", split_axis=0, concat_axis=0, tiled=True),
        lax.all_to_all(
            route_sum.reshape(seq_count * local_experts, CAP),
            "seq",
            split_axis=0,
            concat_axis=0,
            tiled=True,
        ),
    )
    quarter = back_rows.shape[2]
    d_moe_in = jnp.einsum(
        "st,sd->td",
        by_token,
        back_rows.reshape(EXPERTS * CAP, quarter),
        preferred_element_type=jnp.float32,
    ).astype(jnp.bfloat16)
    d_route = jnp.dot(
        back_weight.reshape(EXPERTS * CAP).astype(jnp.float32),
        chosen,
        precision=lax.Precision.HIGHEST,
    )
    d_route_weight = d_route.astype(jnp.bfloat16).reshape(routes.shape)
    return (d_moe_in, d_route_weight, grad_gate, grad_up, grad_down)


def attend(grad_out, d_moe_in, queries, window, first_shard):
    tokens = grad_out.shape[0]
    head_dim = window.shape[1] // 2
    per_group = queries.shape[1] // head_dim
    scale = head_dim ** (-0.5)
    d_hidden = (grad_out.astype(jnp.float32) + d_moe_in.astype(jnp.float32)).astype(jnp.bfloat16)
    query_rows = queries.reshape(tokens * per_group, head_dim)
    grad_rows = d_hidden.reshape(tokens * per_group, head_dim)
    key_rows = window[:, :head_dim]
    value_rows = window[:, head_dim:]
    contract_last = (((1,), (1,)), ((), ()))
    contract_first = (((0,), (0,)), ((), ()))
    seq_index = lax.axis_index("seq")
    key_pos = first_shard * tokens + jnp.arange(window.shape[0], dtype=jnp.int32)
    row_total = tokens * per_group
    block_rows = min(512, row_total)
    block_count = row_total // block_rows

    def attend_block(index, carry):
        d_window, d_query_all = carry
        begin = (index * block_rows).astype(jnp.int32)
        query_blk = lax.dynamic_slice_in_dim(query_rows, begin, block_rows, 0)
        grad_blk = lax.dynamic_slice_in_dim(grad_rows, begin, block_rows, 0)
        scores = (
            lax.dot_general(query_blk, key_rows, contract_last, preferred_element_type=jnp.float32)
            * scale
        )
        position = (
            seq_index * tokens + (begin + jnp.arange(block_rows, dtype=jnp.int32)) // per_group
        )
        visible = (
            (key_pos[None, :] >= 0)
            & (key_pos[None, :] <= position[:, None])
            & (key_pos[None, :] > position[:, None] - WIN)
        )
        scores = jnp.where(visible, scores, -1e30)
        row_max = jnp.max(scores, axis=1, keepdims=True)
        raised = jnp.exp(scores - row_max)
        probs = raised / jnp.sum(raised, axis=1, keepdims=True)
        d_probs = lax.dot_general(
            grad_blk, value_rows, contract_last, preferred_element_type=jnp.float32
        )
        row_dot = jnp.sum(probs * d_probs, axis=1, keepdims=True)
        d_scores = (probs * (d_probs - row_dot) * scale).astype(jnp.bfloat16)
        probs_low = probs.astype(jnp.bfloat16)
        d_query_blk = jnp.dot(d_scores, key_rows, preferred_element_type=jnp.float32).astype(
            jnp.bfloat16
        )
        d_keys = lax.dot_general(
            d_scores, query_blk, contract_first, preferred_element_type=jnp.float32
        )
        d_values = lax.dot_general(
            probs_low, grad_blk, contract_first, preferred_element_type=jnp.float32
        )
        d_window = d_window + jnp.concatenate([d_keys, d_values], axis=1)
        d_query_all = lax.dynamic_update_slice_in_dim(d_query_all, d_query_blk, begin, 0)
        return (d_window, d_query_all)

    window_start = jnp.zeros(window.shape, jnp.float32)
    query_start = jnp.zeros((row_total, head_dim), jnp.bfloat16)
    d_window, d_query_all = lax.fori_loop(0, block_count, attend_block, (window_start, query_start))
    d_queries = d_query_all.reshape(tokens, per_group * head_dim)
    return (d_queries, d_window)


def attention(grad_out, d_moe_in, queries, key_value):
    tokens = grad_out.shape[0]
    reach = min(WIN // tokens, lax.axis_size("seq") - 1)
    window = fetch_window(key_value.reshape(tokens, key_value.shape[2]), reach)
    first_shard = lax.axis_index("seq") - reach
    d_queries, d_window = attend(grad_out, d_moe_in, queries, window, first_shard)
    d_own = return_window(d_window, reach, tokens)
    d_key_value = d_own.astype(jnp.bfloat16).reshape(key_value.shape)
    return (d_queries, d_key_value)


def dot(a, b, contract):
    return lax.dot_general(a, b, (contract, ((), ())), preferred_element_type=jnp.float32)


def expert_kernel(
    tables_ref,
    tokens_ref,
    wg_ref,
    wu_ref,
    wd_ref,
    gg_ref,
    gu_ref,
    gd_ref,
    dmoe_ref,
    routes_ref,
    weight_ref,
    droute_ref,
    rank_ref,
    dense_ref,
    pick_ref,
    back_ref,
):
    group = pl.program_id(0)
    per_step = wg_ref.shape[0]
    _, heads, total, quarter = tokens_ref.shape
    shard_count, double_top, shard = tables_ref.shape
    top = double_top // 2
    hidden = wg_ref.shape[2]
    rows = pick_ref.shape[0] // rank_ref.shape[0]
    local = rank_ref.shape[0]

    @pl.when(group == 0)
    def _():
        first = (lax.axis_index("seq") * local).astype(jnp.float32)
        for s in range(shard_count):
            columns = slice(s * shard, (s + 1) * shard)
            routes_ref[:, columns] = tables_ref[s, :top, :] - first
            weight_ref[:, columns] = tables_ref[s, top:, :]
        for index in range(local):
            hit = routes_ref[...] == index
            named = jnp.sum(hit.astype(jnp.float32), axis=0, keepdims=True)
            rank_ref[pl.ds(index, 1), :] = named
            dense_ref[pl.ds(index, 1), :] = jnp.sum(
                jnp.where(hit, weight_ref[...], 0.0), axis=0, keepdims=True
            )
        named = rank_ref[...]
        before = lax.broadcasted_iota(jnp.int32, (total, total), 0)
        after = lax.broadcasted_iota(jnp.int32, (total, total), 1)
        order = (before < after).astype(jnp.float32).astype(jnp.bfloat16)
        earlier = dot(named.astype(jnp.bfloat16), order, ((1,), (0,)))
        rank_ref[...] = jnp.where(named > 0.5, earlier, -1.0)
        droute_ref[...] = jnp.zeros_like(droute_ref)

    slots = lax.broadcasted_iota(jnp.int32, (rows, total), 0).astype(jnp.float32)

    def choose(j):
        expert = group * per_step + j
        chosen = rank_ref[pl.ds(expert, 1), :] == slots
        pick = chosen.astype(jnp.float32).astype(jnp.bfloat16)
        scale_w = jnp.sum(
            jnp.where(chosen, dense_ref[pl.ds(expert, 1), :], 0.0), axis=1, keepdims=True
        )
        return expert, chosen, pick, scale_w

    choices = [choose(j) for j in range(per_step)]
    picks = jnp.concatenate([pick for _, _, pick, _ in choices], axis=0)
    x_all, dy_all = (
        jnp.concatenate(
            [
                dot(picks, tokens_ref[part, h], ((1,), (0,))).astype(jnp.bfloat16)
                for h in range(heads)
            ],
            axis=1,
        )
        for part in range(2)
    )
    start = pl.multiple_of(group * (per_step * rows), rows)
    pick_ref[pl.ds(start, per_step * rows), :] = picks
    forward = []
    for j, (expert, chosen, _, scale_w) in enumerate(choices):
        x = x_all[j * rows : (j + 1) * rows]
        dy = dy_all[j * rows : (j + 1) * rows]
        w_both = jnp.concatenate([wg_ref[j], wu_ref[j]], axis=1)
        pre = dot(x, w_both, ((1,), (0,)))
        back_proj = dot(dy, wd_ref[j], ((1,), (1,)))
        forward.append((x, dy, w_both, pre, back_proj))
    backward = []
    for (expert, chosen, _, scale_w), (x, dy, w_both, pre, back_proj) in zip(choices, forward):
        gate_pre = pre[:, :hidden]
        up_pre = pre[:, hidden:]
        sigmoid_gate = jax.nn.sigmoid(gate_pre)
        silu_gate = gate_pre * sigmoid_gate
        active = silu_gate * up_pre
        route_part = jnp.sum(active * back_proj, axis=1, keepdims=True)
        route_row = jnp.sum(jnp.where(chosen, route_part, 0.0), axis=0, keepdims=True)
        droute_ref[...] += jnp.where(
            routes_ref[...] == expert.astype(jnp.float32), route_row, 0.0
        )
        d_active = scale_w * back_proj
        d_gate = d_active * up_pre * sigmoid_gate * (1.0 + gate_pre * (1.0 - sigmoid_gate))
        d_up = d_active * silu_gate
        d_both = jnp.concatenate([d_gate, d_up], axis=1).astype(jnp.bfloat16)
        backward.append((d_both, (scale_w * active).astype(jnp.bfloat16)))
    for j, (x, dy, w_both, _, _) in enumerate(forward):
        d_both, weighted = backward[j]
        back_ref[pl.ds(start + j * rows, rows), :] = dot(d_both, w_both, ((1,), (1,))).astype(
            jnp.bfloat16
        )
        grad_both = dot(x, d_both, ((0,), (0,))).astype(jnp.bfloat16)
        gg_ref[j] = grad_both[:, :hidden]
        gu_ref[j] = grad_both[:, hidden:]
        gd_ref[j] = dot(weighted, dy, ((0,), (0,))).astype(jnp.bfloat16)

    @pl.when(group == pl.num_programs(0) - 1)
    def _():
        for h in range(heads):
            columns = slice(h * quarter, (h + 1) * quarter)
            summed = dot(pick_ref[...], back_ref[:, columns], ((0,), (0,))).astype(jnp.bfloat16)
            for s in range(shard_count):
                dmoe_ref[h, s, :shard, :] = summed[s * shard : (s + 1) * shard]
                share = droute_ref[:, s * shard : (s + 1) * shard]
                share = jnp.concatenate([share, jnp.zeros((16 - top, shard), jnp.float32)], axis=0)
                if quarter > shard:
                    blank = jnp.zeros((16, quarter - shard), jnp.float32)
                    share = jnp.concatenate([share, blank], axis=1)
                dmoe_ref[h, s, shard:, :] = share.astype(jnp.bfloat16)


def run_experts(tables, tokens, w_gate, w_up, w_down):
    local, width, hidden = w_gate.shape
    _, heads, total, quarter = tokens.shape
    shard_count, double_top, shard = tables.shape
    top = double_top // 2
    rows = -(-shard_count * CAP // 16) * 16
    whole = lambda *shape: pl.BlockSpec(shape, lambda e: (0,) * len(shape))
    per_step = 2 if local % 2 == 0 else 1
    wide = pl.BlockSpec((per_step, width, hidden), lambda e: (e, 0, 0))
    tall = pl.BlockSpec((per_step, hidden, width), lambda e: (e, 0, 0))
    back_shape = (heads, shard_count, shard + 16, quarter)
    return pl.pallas_call(
        expert_kernel,
        grid=(local // per_step,),
        in_specs=[whole(*tables.shape), whole(*tokens.shape), wide, wide, tall],
        out_specs=[wide, wide, tall, whole(*back_shape)],
        out_shape=[
            jax.ShapeDtypeStruct(w_gate.shape, jnp.bfloat16),
            jax.ShapeDtypeStruct(w_up.shape, jnp.bfloat16),
            jax.ShapeDtypeStruct(w_down.shape, jnp.bfloat16),
            jax.ShapeDtypeStruct(back_shape, jnp.bfloat16),
        ],
        scratch_shapes=[
            pltpu.VMEM((top, total), jnp.float32),
            pltpu.VMEM((top, total), jnp.float32),
            pltpu.VMEM((top, total), jnp.float32),
            pltpu.VMEM((local, total), jnp.float32),
            pltpu.VMEM((local, total), jnp.float32),
            pltpu.VMEM((local * rows, total), jnp.bfloat16),
            pltpu.VMEM((local * rows, width), jnp.bfloat16),
        ],
        compiler_params=pltpu.CompilerParams(vmem_limit_bytes=60 << 20),
        name="experts",
    )(tables, tokens, w_gate, w_up, w_down)


def head_neighbours():
    head = lax.axis_index("head")
    return head, head + 1 - 2 * (head % 2), (head + 2) % 4, (head + 3 - 2 * (head % 2)) % 4


def inside(index, count):
    return (index >= 0) & (index < count)


def greet(along, across):
    seq = lax.axis_index("seq")
    count = lax.axis_size("seq")
    barrier = pltpu.get_barrier_semaphore()
    for peer in across:
        pl.semaphore_signal(barrier, inc=1, device_id={"head": peer}, device_id_type=MESH)
    for step in along:

        @pl.when(inside(seq + step, count))
        def _():
            pl.semaphore_signal(
                barrier, inc=1, device_id={"seq": seq + step}, device_id_type=MESH
            )

    ends = (seq == 0).astype(jnp.int32) + (seq == count - 1).astype(jnp.int32)
    pl.semaphore_wait(barrier, len(across) + len(along) - ends)


def send(source, target, send_sem, recv_sem, peer):
    return pltpu.make_async_remote_copy(
        src_ref=source,
        dst_ref=target,
        send_sem=send_sem,
        recv_sem=recv_sem,
        device_id=peer,
        device_id_type=MESH,
    )


def gather_kernel(
    in_ref,
    grad_ref,
    table_ref,
    kv_ref,
    tokens_ref,
    tables_ref,
    window_ref,
    own_sem,
    line_send,
    line_recv,
    square_send,
    square_recv,
):
    seq = lax.axis_index("seq")
    count = lax.axis_size("seq")
    shard = in_ref.shape[0]
    half = shard // 2
    head, beside, above, corner = head_neighbours()

    def piece(of, p):
        return tokens_ref.at[:, of, pl.ds(p * shard, shard), :]

    def upper(of, p):
        return tokens_ref.at[:, of, pl.ds(p * shard, half), :]

    def lower(of, p):
        return tokens_ref.at[:, of, pl.ds(p * shard + half, half), :]

    own_rows = pl.ds(seq * shard, shard)
    own = [
        pltpu.make_async_copy(in_ref, tokens_ref.at[0, head, own_rows, :], own_sem.at[0]),
        pltpu.make_async_copy(grad_ref, tokens_ref.at[1, head, own_rows, :], own_sem.at[1]),
        pltpu.make_async_copy(table_ref, tables_ref.at[seq], own_sem.at[2]),
        pltpu.make_async_copy(kv_ref, window_ref.at[seq], own_sem.at[3]),
    ]
    for copy in own:
        copy.start()
    greet((-1, 1), (beside, above))
    for copy in own:
        copy.wait()

    def line(way, p, to):
        refs = (piece(head, p), tables_ref.at[p], window_ref.at[p])
        return [
            send(ref, ref, line_send.at[way, j, p], line_recv.at[way, j, p], {"seq": to})
            for j, ref in enumerate(refs)
        ]

    def square(kind, ref, p, to):
        return send(ref, ref, square_send.at[kind, p], square_recv.at[kind, p], {"head": to})

    def forward(p):
        square(0, piece(beside, p), p, beside).wait_recv()
        square(2, upper(beside, p), p, above).start()
        square(1, piece(above, p), p, above).wait_recv()
        square(3, lower(above, p), p, beside).start()

    ways = ((0, 1), (1, -1))
    for k in range(count):
        for way, step in ways:
            p = seq - step * k

            @pl.when(inside(p, count))
            def _():
                if k > 0:
                    for copy in line(way, p, seq - step):
                        copy.wait_recv()

                @pl.when(inside(seq + step, count))
                def _():
                    for copy in line(way, p, seq + step):
                        copy.start()

                if k > 0 or way == 0:
                    square(0, piece(head, p), p, beside).start()
                    square(1, piece(head, p), p, above).start()

        if k > 0:
            for way, step in ways:
                if k > 1 or way == 0:
                    p = seq - step * (k - 1)
                    pl.when(inside(p, count))(lambda p=p: forward(p))
    for way, step in ways:
        if count > 1 or way == 0:
            p = seq - step * (count - 1)
            pl.when(inside(p, count))(lambda p=p: forward(p))
    for p in range(count):
        square(2, upper(corner, p), p, above).wait_recv()
        square(3, lower(corner, p), p, beside).wait_recv()
        square(0, piece(head, p), p, beside).wait_send()
        square(1, piece(head, p), p, above).wait_send()
        square(2, upper(beside, p), p, above).wait_send()
        square(3, lower(above, p), p, beside).wait_send()
    for k in range(count):
        for way, step in ways:
            p = seq - step * k

            @pl.when(inside(p, count) & inside(seq + step, count))
            def _():
                for copy in line(way, p, seq + step):
                    copy.wait_send()


def gather_tokens(moe_in, grad_out, table, key_value):
    heads = lax.axis_size("head")
    count = lax.axis_size("seq")
    shard, quarter = moe_in.shape
    return pl.pallas_call(
        gather_kernel,
        in_specs=[pl.BlockSpec(memory_space=pltpu.VMEM)] * 4,
        out_specs=[pl.BlockSpec(memory_space=pltpu.VMEM)] * 3,
        out_shape=[
            jax.ShapeDtypeStruct((2, heads, count * shard, quarter), jnp.bfloat16),
            jax.ShapeDtypeStruct((count,) + table.shape, jnp.float32),
            jax.ShapeDtypeStruct((count,) + key_value.shape, jnp.bfloat16),
        ],
        scratch_shapes=[
            pltpu.SemaphoreType.DMA((4,)),
            pltpu.SemaphoreType.DMA((2, 3, count)),
            pltpu.SemaphoreType.DMA((2, 3, count)),
            pltpu.SemaphoreType.DMA((4, count)),
            pltpu.SemaphoreType.DMA((4, count)),
        ],
        compiler_params=pltpu.CompilerParams(collective_id=0, has_side_effects=True),
        name="gather_tokens",
    )(moe_in, grad_out, table, key_value)


def reduce_kernel(
    part_ref,
    total_ref,
    beside_half,
    above_half,
    beside_full,
    above_full,
    to_beside,
    to_above,
    to_line,
    from_line,
    send_sem,
    recv_sem,
):
    seq = lax.axis_index("seq")
    count = lax.axis_size("seq")
    half = beside_half.shape[1]
    head, beside, above, corner = head_neighbours()
    greet((-1, 1), (beside, above))

    def pair(kind, source, target, p, peer):
        return send(source, target, send_sem.at[kind, p], recv_sem.at[kind, p], peer)

    def first(p):
        return (
            pair(
                0,
                part_ref.at[corner, p, pl.ds(0, half), :],
                beside_half.at[p],
                p,
                {"head": beside},
            ),
            pair(
                1,
                part_ref.at[corner, p, pl.ds(half, part_ref.shape[2] - half), :],
                above_half.at[p],
                p,
                {"head": above},
            ),
        )

    def second(p):
        return (
            pair(2, to_beside.at[p], beside_full.at[p], p, {"head": beside}),
            pair(3, to_above.at[p], above_full.at[p], p, {"head": above}),
        )

    def line(way, p, to):
        return pair(4 + way, to_line.at[p], from_line.at[way, p], p, {"seq": to})

    def each(body):
        for k in reversed(range(count)):
            for way, step in ((0, 1), (1, -1)):
                if k > 0 or way == 0:
                    p = seq + step * k
                    pl.when(inside(p, count))(lambda k=k, way=way, step=step, p=p: body(k, way, step, p))

    def start_first(k, way, step, p):
        for copy in first(p):
            copy.start()

    def add_first(k, way, step, p):
        from_beside, from_above = first(p)
        via_beside, via_above = second(p)
        from_beside.wait_recv()
        to_above[p, :half, :] = (
            part_ref[above, p, :half, :].astype(jnp.float32)
            + beside_half[p].astype(jnp.float32)
        ).astype(jnp.bfloat16)
        to_above[p, half:, :] = part_ref[above, p, half:, :]
        via_above.start()
        from_above.wait_recv()
        to_beside[p, :half, :] = part_ref[beside, p, :half, :]
        to_beside[p, half:, :] = (
            part_ref[beside, p, half:, :].astype(jnp.float32) + above_half[p].astype(jnp.float32)
        ).astype(jnp.bfloat16)
        via_beside.start()

    def add_second(k, way, step, p):
        for copy in second(p):
            copy.wait_recv()
        summed = (
            part_ref[head, p].astype(jnp.float32)
            + beside_full[p].astype(jnp.float32)
            + above_full[p].astype(jnp.float32)
        )
        if k > 0:
            to_line[p] = summed.astype(jnp.bfloat16)

            @pl.when(inside(seq - step, count))
            def _():
                line(way, p, seq - step).wait_recv()
                to_line[p] = (summed + from_line[way, p].astype(jnp.float32)).astype(jnp.bfloat16)

            line(way, p, seq + step).start()
        else:
            for other in range(count):

                @pl.when(seq == other)
                def _():
                    result = summed
                    if other > 0:
                        line(0, p, seq - 1).wait_recv()
                        result = result + from_line[0, p].astype(jnp.float32)
                    if other < count - 1:
                        line(1, p, seq + 1).wait_recv()
                        result = result + from_line[1, p].astype(jnp.float32)
                    total_ref[...] = result.astype(jnp.bfloat16)

    def finish(k, way, step, p):
        for copy in first(p) + second(p):
            copy.wait_send()
        if k > 0:
            line(way, p, seq + step).wait_send()

    each(start_first)
    each(add_first)
    each(add_second)
    each(finish)


def reduce_tokens(part):
    _, count, rows, quarter = part.shape
    half = (rows - 16) // 2
    block = lambda *lead: pltpu.VMEM(lead + (rows, quarter), jnp.bfloat16)
    return pl.pallas_call(
        reduce_kernel,
        in_specs=[pl.BlockSpec(memory_space=pltpu.VMEM)],
        out_specs=pl.BlockSpec(memory_space=pltpu.VMEM),
        out_shape=jax.ShapeDtypeStruct((rows, quarter), jnp.bfloat16),
        scratch_shapes=[
            pltpu.VMEM((count, half, quarter), jnp.bfloat16),
            pltpu.VMEM((count, rows - half, quarter), jnp.bfloat16),
            block(count),
            block(count),
            block(count),
            block(count),
            block(count),
            block(2, count),
            pltpu.SemaphoreType.DMA((6, count)),
            pltpu.SemaphoreType.DMA((6, count)),
        ],
        compiler_params=pltpu.CompilerParams(collective_id=1, has_side_effects=True),
        name="reduce_tokens",
    )(part)


def attend_kernel(
    grad_ref,
    summed_ref,
    query_ref,
    window_ref,
    d_query_ref,
    total_ref,
    part_ref,
    landed,
    send_sem,
    recv_sem,
):
    seq = lax.axis_index("seq")
    count, shard, width = window_ref.shape
    head_dim = width // 2
    per_group = query_ref.shape[1] // head_dim
    scale = head_dim ** (-0.5)
    barrier = pltpu.get_barrier_semaphore()
    for offset in range(1, count):
        pl.semaphore_signal(
            barrier, inc=1, device_id={"seq": (seq + offset) % count}, device_id_type=MESH
        )
    window = jnp.concatenate([window_ref[p] for p in range(count)], axis=0)
    key_rows = window[:, :head_dim]
    value_rows = window[:, head_dim:]
    d_hidden = (
        grad_ref[...].astype(jnp.float32) + summed_ref[:shard, :].astype(jnp.float32)
    ).astype(jnp.bfloat16)
    position = seq * shard + lax.broadcasted_iota(jnp.int32, (shard, count * shard), 0)
    key_pos = lax.broadcasted_iota(jnp.int32, (shard, count * shard), 1)
    visible = (key_pos <= position) & (key_pos > position - WIN)
    d_keys = jnp.zeros((head_dim, count * shard), jnp.float32)
    d_values = jnp.zeros((head_dim, count * shard), jnp.float32)
    d_query = []
    for g in range(per_group):
        columns = slice(g * head_dim, (g + 1) * head_dim)
        query = query_ref[:, columns]
        grad = d_hidden[:, columns]
        scores = dot(query, key_rows, ((1,), (1,))) * scale
        scores = jnp.where(visible, scores, -1e30)
        raised = jnp.exp(scores - jnp.max(scores, axis=1, keepdims=True))
        probs = raised / jnp.sum(raised, axis=1, keepdims=True)
        d_probs = dot(grad, value_rows, ((1,), (1,)))
        row_dot = jnp.sum(probs * d_probs, axis=1, keepdims=True)
        d_scores = (probs * (d_probs - row_dot) * scale).astype(jnp.bfloat16)
        d_query.append(dot(d_scores, key_rows, ((1,), (0,))).astype(jnp.bfloat16))
        d_keys = d_keys + dot(query, d_scores, ((0,), (0,)))
        d_values = d_values + dot(grad, probs.astype(jnp.bfloat16), ((0,), (0,)))
    d_window = jnp.concatenate([d_keys, d_values], axis=0).T.astype(jnp.bfloat16)
    for p in range(count):
        part_ref[p] = d_window[p * shard : (p + 1) * shard]
    pl.semaphore_wait(barrier, count - 1)
    copies = []
    for offset in range(1, count):
        to = (seq + offset) % count
        copies.append(
            send(
                part_ref.at[to],
                landed.at[offset],
                send_sem.at[offset],
                recv_sem.at[offset],
                {"seq": to},
            )
        )
        copies[-1].start()
    d_query_ref[...] = jnp.concatenate(d_query, axis=1)
    summed = part_ref[seq].astype(jnp.float32)
    for offset, copy in enumerate(copies, 1):
        copy.wait_recv()
        summed = summed + landed[offset].astype(jnp.float32)
    total_ref[...] = summed.astype(jnp.bfloat16)
    for copy in copies:
        copy.wait_send()


def attend_and_return(grad_out, summed, queries, window):
    count, shard, width = window.shape
    return pl.pallas_call(
        attend_kernel,
        in_specs=[pl.BlockSpec(memory_space=pltpu.VMEM)] * 4,
        out_specs=[pl.BlockSpec(memory_space=pltpu.VMEM)] * 2,
        out_shape=[
            jax.ShapeDtypeStruct(queries.shape, jnp.bfloat16),
            jax.ShapeDtypeStruct((shard, width), jnp.bfloat16),
        ],
        scratch_shapes=[
            pltpu.VMEM(window.shape, jnp.bfloat16),
            pltpu.VMEM(window.shape, jnp.bfloat16),
            pltpu.SemaphoreType.DMA((count,)),
            pltpu.SemaphoreType.DMA((count,)),
        ],
        compiler_params=pltpu.CompilerParams(collective_id=2, has_side_effects=True),
        name="attend_and_return",
    )(grad_out, summed, queries, window)


def gathered_layer(moe_in, grad_out, routes, route_weight, w_gate, w_up, w_down, queries, key_value):
    shard, top = routes.shape
    table = jnp.concatenate(
        [routes.astype(jnp.float32).T, route_weight.astype(jnp.float32).T], axis=0
    )
    own_rows = key_value.reshape(shard, key_value.shape[2])
    tokens, tables, window = gather_tokens(moe_in, grad_out, table, own_rows)
    grad_gate, grad_up, grad_down, d_moe = run_experts(tables, tokens, w_gate, w_up, w_down)
    summed = reduce_tokens(d_moe)
    d_moe_in = summed[:shard]
    d_route_weight = summed[shard : shard + top, :shard].T
    d_queries, d_own = attend_and_return(grad_out, summed, queries, window)
    d_key_value = d_own.reshape(key_value.shape)
    return (d_moe_in, d_route_weight, grad_gate, grad_up, grad_down, d_queries, d_key_value)


def shards(moe_in, grad_out, routes, route_weight, w_gate, w_up, w_down, queries, key_value):
    gathered_rows = lax.axis_size("seq") * moe_in.shape[0]
    if gathered_rows <= EXPERTS * CAP and lax.axis_size("head") == 4:
        return gathered_layer(
            moe_in, grad_out, routes, route_weight, w_gate, w_up, w_down, queries, key_value
        )
    d_moe_in, d_route_weight, grad_gate, grad_up, grad_down = dispatched_experts(
        moe_in, grad_out, routes, route_weight, w_gate, w_up, w_down
    )
    d_queries, d_key_value = attention(grad_out, d_moe_in, queries, key_value)
    return (d_moe_in, d_route_weight, grad_gate, grad_up, grad_down, d_queries, d_key_value)


def solution(mesh):
    in_specs = (
        P(("rep", "seq"), "head"),
        P(("rep", "seq"), "head"),
        P(("rep", "seq"), None),
        P(("rep", "seq"), None),
        P("seq", None, "head"),
        P("seq", None, "head"),
        P("seq", "head", None),
        P(("rep", "seq"), "head"),
        P(("rep", "seq"), "head", None),
    )
    out_specs = (
        P(("rep", "seq"), "head"),
        P(("rep", "seq"), None),
        P(("rep", "seq"), None, "head"),
        P(("rep", "seq"), None, "head"),
        P(("rep", "seq"), "head", None),
        P(("rep", "seq"), "head"),
        P(("rep", "seq"), "head", None),
    )
    return jax.shard_map(shards, mesh=mesh, in_specs=in_specs, out_specs=out_specs, check_vma=False)
```

```python
import jax
import jax.numpy as jnp
from jax import lax
from jax.experimental import pallas as pl
from jax.experimental.pallas import tpu as pltpu
from jax.sharding import PartitionSpec as P

EXPERTS = 64
WIN = 512
CAP = 18
MESH = pl.DeviceIdType.MESH


def shifted(block, axis, distance):
    devices = range(lax.axis_size(axis))
    route = [(i - distance, i) for i in devices if i - distance in devices]
    return lax.ppermute(block, axis, route)


def slot_tables(routes, route_weight):
    token_rows, top_count = routes.shape
    flat_expert = routes.reshape(token_rows * top_count)
    expert_ids = jnp.arange(EXPERTS, dtype=jnp.int32)
    one_hot = (flat_expert[:, None] == expert_ids[None, :]).astype(jnp.int32)
    earlier = jnp.cumsum(one_hot, axis=0) - one_hot
    slot_rank = jnp.sum(earlier * one_hot, axis=1)
    target = flat_expert * CAP + slot_rank
    slot_cells = jnp.arange(EXPERTS * CAP, dtype=jnp.int32)
    chosen = (target[None, :] == slot_cells[:, None]).astype(jnp.float32)
    by_token = jnp.sum(chosen.reshape(EXPERTS * CAP, token_rows, top_count), axis=2).astype(
        jnp.bfloat16
    )
    slot_weight = jnp.dot(
        chosen,
        route_weight.reshape(token_rows * top_count).astype(jnp.float32),
        precision=lax.Precision.HIGHEST,
    )
    return (chosen, by_token, slot_weight.astype(jnp.bfloat16).reshape(EXPERTS, CAP))


def place_rows(by_token, source):
    placed = jnp.dot(by_token, source, preferred_element_type=jnp.float32)
    return placed.astype(jnp.bfloat16).reshape(EXPERTS, CAP, source.shape[1])


def fetch_window(own_rows, reach):
    earlier_shards = [shifted(own_rows, "seq", offset) for offset in range(reach, 0, -1)]
    window = jnp.concatenate(earlier_shards + [own_rows], axis=0)
    return window


def return_window(d_window, reach, shard):
    summed = d_window[reach * shard :]
    for offset in range(1, reach + 1):
        begin = (reach - offset) * shard
        summed = summed + shifted(
            d_window[begin : begin + shard].astype(jnp.bfloat16), "seq", -offset
        ).astype(jnp.float32)
    return summed


def dispatched_experts(moe_in, grad_out, routes, route_weight, w_gate, w_up, w_down):
    seq_count = lax.axis_size("seq")
    local_experts = w_gate.shape[0]
    chosen, by_token, slot_weight = slot_tables(routes, route_weight)
    part_in, part_grad, got_weight = (
        lax.all_to_all(
            place_rows(by_token, moe_in), "seq", split_axis=0, concat_axis=0, tiled=True
        ),
        lax.all_to_all(
            place_rows(by_token, grad_out), "seq", split_axis=0, concat_axis=0, tiled=True
        ),
        lax.all_to_all(slot_weight, "seq", split_axis=0, concat_axis=0, tiled=True),
    )
    got_in, got_grad = (
        lax.all_gather(part_in, "head", axis=2, tiled=True),
        lax.all_gather(part_grad, "head", axis=2, tiled=True),
    )
    width = got_in.shape[2]
    rows_in = got_in.reshape(seq_count, local_experts, CAP, width)
    rows_grad = got_grad.reshape(seq_count, local_experts, CAP, width)
    scale_w = got_weight.reshape(seq_count, local_experts, CAP).astype(jnp.float32)[..., None]
    gate_pre = jnp.einsum("secd,edf->secf", rows_in, w_gate, preferred_element_type=jnp.float32)
    up_pre = jnp.einsum("secd,edf->secf", rows_in, w_up, preferred_element_type=jnp.float32)
    back_proj = jnp.einsum("secd,efd->secf", rows_grad, w_down, preferred_element_type=jnp.float32)
    sigmoid_gate = jax.nn.sigmoid(gate_pre)
    silu_gate = gate_pre * sigmoid_gate
    active = silu_gate * up_pre
    route_part = jnp.sum(active * back_proj, axis=3)
    d_active = scale_w * back_proj
    d_gate = (d_active * up_pre * sigmoid_gate * (1.0 + gate_pre * (1.0 - sigmoid_gate))).astype(
        jnp.bfloat16
    )
    d_up = (d_active * silu_gate).astype(jnp.bfloat16)
    weighted = (scale_w * active).astype(jnp.bfloat16)
    rows_back = jnp.einsum("secf,edf->secd", d_gate, w_gate, preferred_element_type=jnp.float32)
    rows_back = rows_back + jnp.einsum(
        "secf,edf->secd", d_up, w_up, preferred_element_type=jnp.float32
    )
    rows_quarter = lax.psum_scatter(
        rows_back.reshape(seq_count * local_experts, CAP, width).astype(jnp.bfloat16),
        "head",
        scatter_dimension=2,
        tiled=True,
    )
    route_sum = lax.psum(route_part, "head").astype(jnp.bfloat16)
    grad_gate = jnp.einsum(
        "secd,secf->edf", rows_in, d_gate, preferred_element_type=jnp.float32
    ).astype(jnp.bfloat16)
    grad_up = jnp.einsum(
        "secd,secf->edf", rows_in, d_up, preferred_element_type=jnp.float32
    ).astype(jnp.bfloat16)
    grad_down = jnp.einsum(
        "secf,secd->efd", weighted, rows_grad, preferred_element_type=jnp.float32
    ).astype(jnp.bfloat16)
    back_rows, back_weight = (
        lax.all_to_all(rows_quarter, "seq", split_axis=0, concat_axis=0, tiled=True),
        lax.all_to_all(
            route_sum.reshape(seq_count * local_experts, CAP),
            "seq",
            split_axis=0,
            concat_axis=0,
            tiled=True,
        ),
    )
    quarter = back_rows.shape[2]
    d_moe_in = jnp.einsum(
        "st,sd->td",
        by_token,
        back_rows.reshape(EXPERTS * CAP, quarter),
        preferred_element_type=jnp.float32,
    ).astype(jnp.bfloat16)
    d_route = jnp.dot(
        back_weight.reshape(EXPERTS * CAP).astype(jnp.float32),
        chosen,
        precision=lax.Precision.HIGHEST,
    )
    d_route_weight = d_route.astype(jnp.bfloat16).reshape(routes.shape)
    return (d_moe_in, d_route_weight, grad_gate, grad_up, grad_down)


def attend(grad_out, d_moe_in, queries, window, first_shard):
    tokens = grad_out.shape[0]
    head_dim = window.shape[1] // 2
    per_group = queries.shape[1] // head_dim
    scale = head_dim ** (-0.5)
    d_hidden = (grad_out.astype(jnp.float32) + d_moe_in.astype(jnp.float32)).astype(jnp.bfloat16)
    query_rows = queries.reshape(tokens * per_group, head_dim)
    grad_rows = d_hidden.reshape(tokens * per_group, head_dim)
    key_rows = window[:, :head_dim]
    value_rows = window[:, head_dim:]
    contract_last = (((1,), (1,)), ((), ()))
    contract_first = (((0,), (0,)), ((), ()))
    seq_index = lax.axis_index("seq")
    key_pos = first_shard * tokens + jnp.arange(window.shape[0], dtype=jnp.int32)
    row_total = tokens * per_group
    block_rows = min(512, row_total)
    block_count = row_total // block_rows

    def attend_block(index, carry):
        d_window, d_query_all = carry
        begin = (index * block_rows).astype(jnp.int32)
        query_blk = lax.dynamic_slice_in_dim(query_rows, begin, block_rows, 0)
        grad_blk = lax.dynamic_slice_in_dim(grad_rows, begin, block_rows, 0)
        scores = (
            lax.dot_general(query_blk, key_rows, contract_last, preferred_element_type=jnp.float32)
            * scale
        )
        position = (
            seq_index * tokens + (begin + jnp.arange(block_rows, dtype=jnp.int32)) // per_group
        )
        visible = (
            (key_pos[None, :] >= 0)
            & (key_pos[None, :] <= position[:, None])
            & (key_pos[None, :] > position[:, None] - WIN)
        )
        scores = jnp.where(visible, scores, -1e30)
        row_max = jnp.max(scores, axis=1, keepdims=True)
        raised = jnp.exp(scores - row_max)
        probs = raised / jnp.sum(raised, axis=1, keepdims=True)
        d_probs = lax.dot_general(
            grad_blk, value_rows, contract_last, preferred_element_type=jnp.float32
        )
        row_dot = jnp.sum(probs * d_probs, axis=1, keepdims=True)
        d_scores = (probs * (d_probs - row_dot) * scale).astype(jnp.bfloat16)
        probs_low = probs.astype(jnp.bfloat16)
        d_query_blk = jnp.dot(d_scores, key_rows, preferred_element_type=jnp.float32).astype(
            jnp.bfloat16
        )
        d_keys = lax.dot_general(
            d_scores, query_blk, contract_first, preferred_element_type=jnp.float32
        )
        d_values = lax.dot_general(
            probs_low, grad_blk, contract_first, preferred_element_type=jnp.float32
        )
        d_window = d_window + jnp.concatenate([d_keys, d_values], axis=1)
        d_query_all = lax.dynamic_update_slice_in_dim(d_query_all, d_query_blk, begin, 0)
        return (d_window, d_query_all)

    window_start = jnp.zeros(window.shape, jnp.float32)
    query_start = jnp.zeros((row_total, head_dim), jnp.bfloat16)
    d_window, d_query_all = lax.fori_loop(0, block_count, attend_block, (window_start, query_start))
    d_queries = d_query_all.reshape(tokens, per_group * head_dim)
    return (d_queries, d_window)


def attention(grad_out, d_moe_in, queries, key_value):
    tokens = grad_out.shape[0]
    reach = min(WIN // tokens, lax.axis_size("seq") - 1)
    window = fetch_window(key_value.reshape(tokens, key_value.shape[2]), reach)
    first_shard = lax.axis_index("seq") - reach
    d_queries, d_window = attend(grad_out, d_moe_in, queries, window, first_shard)
    d_own = return_window(d_window, reach, tokens)
    d_key_value = d_own.astype(jnp.bfloat16).reshape(key_value.shape)
    return (d_queries, d_key_value)


def dot(a, b, contract):
    return lax.dot_general(a, b, (contract, ((), ())), preferred_element_type=jnp.float32)


def expert_kernel(
    tables_ref,
    tokens_ref,
    wg_ref,
    wu_ref,
    wd_ref,
    gg_ref,
    gu_ref,
    gd_ref,
    dmoe_ref,
    routes_ref,
    weight_ref,
    droute_ref,
    rank_ref,
    dense_ref,
    pick_ref,
    back_ref,
):
    group = pl.program_id(0)
    per_step = wg_ref.shape[0]
    _, heads, total, quarter = tokens_ref.shape
    shard_count, double_top, shard = tables_ref.shape
    top = double_top // 2
    hidden = wg_ref.shape[2]
    rows = pick_ref.shape[0] // rank_ref.shape[0]
    local = rank_ref.shape[0]

    @pl.when(group == 0)
    def _():
        first = (lax.axis_index("seq") * local).astype(jnp.float32)
        for s in range(shard_count):
            columns = slice(s * shard, (s + 1) * shard)
            routes_ref[:, columns] = tables_ref[s, :top, :] - first
            weight_ref[:, columns] = tables_ref[s, top:, :]
        for index in range(local):
            hit = routes_ref[...] == index
            named = jnp.sum(hit.astype(jnp.float32), axis=0, keepdims=True)
            rank_ref[pl.ds(index, 1), :] = named
            dense_ref[pl.ds(index, 1), :] = jnp.sum(
                jnp.where(hit, weight_ref[...], 0.0), axis=0, keepdims=True
            )
        named = rank_ref[...]
        before = lax.broadcasted_iota(jnp.int32, (total, total), 0)
        after = lax.broadcasted_iota(jnp.int32, (total, total), 1)
        order = (before < after).astype(jnp.float32).astype(jnp.bfloat16)
        earlier = dot(named.astype(jnp.bfloat16), order, ((1,), (0,)))
        rank_ref[...] = jnp.where(named > 0.5, earlier, -1.0)
        droute_ref[...] = jnp.zeros_like(droute_ref)

    slots = lax.broadcasted_iota(jnp.int32, (rows, total), 0).astype(jnp.float32)

    def choose(j):
        expert = group * per_step + j
        chosen = rank_ref[pl.ds(expert, 1), :] == slots
        pick = chosen.astype(jnp.float32).astype(jnp.bfloat16)
        scale_w = jnp.sum(
            jnp.where(chosen, dense_ref[pl.ds(expert, 1), :], 0.0), axis=1, keepdims=True
        )
        return expert, chosen, pick, scale_w

    choices = [choose(j) for j in range(per_step)]
    picks = jnp.concatenate([pick for _, _, pick, _ in choices], axis=0)
    x_all, dy_all = (
        jnp.concatenate(
            [
                dot(picks, tokens_ref[part, h], ((1,), (0,))).astype(jnp.bfloat16)
                for h in range(heads)
            ],
            axis=1,
        )
        for part in range(2)
    )
    start = pl.multiple_of(group * (per_step * rows), rows)
    pick_ref[pl.ds(start, per_step * rows), :] = picks
    forward = []
    for j, (expert, chosen, _, scale_w) in enumerate(choices):
        x = x_all[j * rows : (j + 1) * rows]
        dy = dy_all[j * rows : (j + 1) * rows]
        w_both = jnp.concatenate([wg_ref[j], wu_ref[j]], axis=1)
        pre = dot(x, w_both, ((1,), (0,)))
        back_proj = dot(dy, wd_ref[j], ((1,), (1,)))
        forward.append((x, dy, w_both, pre, back_proj))
    backward = []
    for (expert, chosen, _, scale_w), (x, dy, w_both, pre, back_proj) in zip(choices, forward):
        gate_pre = pre[:, :hidden]
        up_pre = pre[:, hidden:]
        sigmoid_gate = jax.nn.sigmoid(gate_pre)
        silu_gate = gate_pre * sigmoid_gate
        active = silu_gate * up_pre
        route_part = jnp.sum(active * back_proj, axis=1, keepdims=True)
        route_row = jnp.sum(jnp.where(chosen, route_part, 0.0), axis=0, keepdims=True)
        droute_ref[...] += jnp.where(
            routes_ref[...] == expert.astype(jnp.float32), route_row, 0.0
        )
        d_active = scale_w * back_proj
        d_gate = d_active * up_pre * sigmoid_gate * (1.0 + gate_pre * (1.0 - sigmoid_gate))
        d_up = d_active * silu_gate
        d_both = jnp.concatenate([d_gate, d_up], axis=1).astype(jnp.bfloat16)
        backward.append((d_both, (scale_w * active).astype(jnp.bfloat16)))
    for j, (x, dy, w_both, _, _) in enumerate(forward):
        d_both, weighted = backward[j]
        back_ref[pl.ds(start + j * rows, rows), :] = dot(d_both, w_both, ((1,), (1,))).astype(
            jnp.bfloat16
        )
        grad_both = dot(x, d_both, ((0,), (0,))).astype(jnp.bfloat16)
        gg_ref[j] = grad_both[:, :hidden]
        gu_ref[j] = grad_both[:, hidden:]
        gd_ref[j] = dot(weighted, dy, ((0,), (0,))).astype(jnp.bfloat16)

    @pl.when(group == pl.num_programs(0) - 1)
    def _():
        for h in range(heads):
            columns = slice(h * quarter, (h + 1) * quarter)
            summed = dot(pick_ref[...], back_ref[:, columns], ((0,), (0,))).astype(jnp.bfloat16)
            for s in range(shard_count):
                dmoe_ref[h, s, :shard, :] = summed[s * shard : (s + 1) * shard]
                share = droute_ref[:, s * shard : (s + 1) * shard]
                share = jnp.concatenate([share, jnp.zeros((16 - top, shard), jnp.float32)], axis=0)
                if quarter > shard:
                    blank = jnp.zeros((16, quarter - shard), jnp.float32)
                    share = jnp.concatenate([share, blank], axis=1)
                dmoe_ref[h, s, shard:, :] = share.astype(jnp.bfloat16)


def run_experts(tables, tokens, w_gate, w_up, w_down):
    local, width, hidden = w_gate.shape
    _, heads, total, quarter = tokens.shape
    shard_count, double_top, shard = tables.shape
    top = double_top // 2
    rows = -(-shard_count * CAP // 16) * 16
    whole = lambda *shape: pl.BlockSpec(shape, lambda e: (0,) * len(shape))
    per_step = 4 if local % 4 == 0 else 1
    wide = pl.BlockSpec((per_step, width, hidden), lambda e: (e, 0, 0))
    tall = pl.BlockSpec((per_step, hidden, width), lambda e: (e, 0, 0))
    back_shape = (heads, shard_count, shard + 16, quarter)
    return pl.pallas_call(
        expert_kernel,
        grid=(local // per_step,),
        in_specs=[whole(*tables.shape), whole(*tokens.shape), wide, wide, tall],
        out_specs=[wide, wide, tall, whole(*back_shape)],
        out_shape=[
            jax.ShapeDtypeStruct(w_gate.shape, jnp.bfloat16),
            jax.ShapeDtypeStruct(w_up.shape, jnp.bfloat16),
            jax.ShapeDtypeStruct(w_down.shape, jnp.bfloat16),
            jax.ShapeDtypeStruct(back_shape, jnp.bfloat16),
        ],
        scratch_shapes=[
            pltpu.VMEM((top, total), jnp.float32),
            pltpu.VMEM((top, total), jnp.float32),
            pltpu.VMEM((top, total), jnp.float32),
            pltpu.VMEM((local, total), jnp.float32),
            pltpu.VMEM((local, total), jnp.float32),
            pltpu.VMEM((local * rows, total), jnp.bfloat16),
            pltpu.VMEM((local * rows, width), jnp.bfloat16),
        ],
        compiler_params=pltpu.CompilerParams(vmem_limit_bytes=60 << 20),
        name="experts",
    )(tables, tokens, w_gate, w_up, w_down)


def head_neighbours():
    head = lax.axis_index("head")
    return head, head + 1 - 2 * (head % 2), (head + 2) % 4, (head + 3 - 2 * (head % 2)) % 4


def inside(index, count):
    return (index >= 0) & (index < count)


def greet(along, across):
    seq = lax.axis_index("seq")
    count = lax.axis_size("seq")
    barrier = pltpu.get_barrier_semaphore()
    for peer in across:
        pl.semaphore_signal(barrier, inc=1, device_id={"head": peer}, device_id_type=MESH)
    for step in along:

        @pl.when(inside(seq + step, count))
        def _():
            pl.semaphore_signal(
                barrier, inc=1, device_id={"seq": seq + step}, device_id_type=MESH
            )

    ends = (seq == 0).astype(jnp.int32) + (seq == count - 1).astype(jnp.int32)
    pl.semaphore_wait(barrier, len(across) + len(along) - ends)


def send(source, target, send_sem, recv_sem, peer):
    return pltpu.make_async_remote_copy(
        src_ref=source,
        dst_ref=target,
        send_sem=send_sem,
        recv_sem=recv_sem,
        device_id=peer,
        device_id_type=MESH,
    )


def gather_kernel(
    in_ref,
    grad_ref,
    table_ref,
    kv_ref,
    tokens_ref,
    tables_ref,
    window_ref,
    own_sem,
    line_send,
    line_recv,
    square_send,
    square_recv,
):
    seq = lax.axis_index("seq")
    count = lax.axis_size("seq")
    shard = in_ref.shape[0]
    half = shard // 2
    head, beside, above, corner = head_neighbours()

    def piece(of, p):
        return tokens_ref.at[:, of, pl.ds(p * shard, shard), :]

    def upper(of, p):
        return tokens_ref.at[:, of, pl.ds(p * shard, half), :]

    def lower(of, p):
        return tokens_ref.at[:, of, pl.ds(p * shard + half, half), :]

    own_rows = pl.ds(seq * shard, shard)
    own = [
        pltpu.make_async_copy(in_ref, tokens_ref.at[0, head, own_rows, :], own_sem.at[0]),
        pltpu.make_async_copy(grad_ref, tokens_ref.at[1, head, own_rows, :], own_sem.at[1]),
        pltpu.make_async_copy(table_ref, tables_ref.at[seq], own_sem.at[2]),
        pltpu.make_async_copy(kv_ref, window_ref.at[seq], own_sem.at[3]),
    ]
    for copy in own:
        copy.start()
    greet((-1, 1), (beside, above))
    for copy in own:
        copy.wait()

    def line(way, p, to):
        refs = (piece(head, p), tables_ref.at[p], window_ref.at[p])
        return [
            send(ref, ref, line_send.at[way, j, p], line_recv.at[way, j, p], {"seq": to})
            for j, ref in enumerate(refs)
        ]

    def square(kind, ref, p, to):
        return send(ref, ref, square_send.at[kind, p], square_recv.at[kind, p], {"head": to})

    def forward(p):
        square(0, piece(beside, p), p, beside).wait_recv()
        square(2, upper(beside, p), p, above).start()
        square(1, piece(above, p), p, above).wait_recv()
        square(3, lower(above, p), p, beside).start()

    ways = ((0, 1), (1, -1))
    for k in range(count):
        if k == 1:
            forward(seq)
        for way, step in ways:
            p = seq - step * k

            @pl.when(inside(p, count))
            def _():
                if k > 0:
                    for copy in line(way, p, seq - step):
                        copy.wait_recv()

                @pl.when(inside(seq + step, count))
                def _():
                    for copy in line(way, p, seq + step):
                        copy.start()

                if k > 0 or way == 0:
                    square(0, piece(head, p), p, beside).start()
                    square(1, piece(head, p), p, above).start()

        if k > 1:
            for way, step in ways:
                if k > 1 or way == 0:
                    p = seq - step * (k - 1)
                    pl.when(inside(p, count))(lambda p=p: forward(p))
    for way, step in ways:
        if count > 1 or way == 0:
            p = seq - step * (count - 1)
            pl.when(inside(p, count))(lambda p=p: forward(p))
    for p in range(count):
        square(2, upper(corner, p), p, above).wait_recv()
        square(3, lower(corner, p), p, beside).wait_recv()
        square(0, piece(head, p), p, beside).wait_send()
        square(1, piece(head, p), p, above).wait_send()
        square(2, upper(beside, p), p, above).wait_send()
        square(3, lower(above, p), p, beside).wait_send()
    for k in range(count):
        for way, step in ways:
            p = seq - step * k

            @pl.when(inside(p, count) & inside(seq + step, count))
            def _():
                for copy in line(way, p, seq + step):
                    copy.wait_send()


def gather_tokens(moe_in, grad_out, table, key_value):
    heads = lax.axis_size("head")
    count = lax.axis_size("seq")
    shard, quarter = moe_in.shape
    return pl.pallas_call(
        gather_kernel,
        in_specs=[pl.BlockSpec(memory_space=pltpu.VMEM)] * 4,
        out_specs=[pl.BlockSpec(memory_space=pltpu.VMEM)] * 3,
        out_shape=[
            jax.ShapeDtypeStruct((2, heads, count * shard, quarter), jnp.bfloat16),
            jax.ShapeDtypeStruct((count,) + table.shape, jnp.float32),
            jax.ShapeDtypeStruct((count,) + key_value.shape, jnp.bfloat16),
        ],
        scratch_shapes=[
            pltpu.SemaphoreType.DMA((4,)),
            pltpu.SemaphoreType.DMA((2, 3, count)),
            pltpu.SemaphoreType.DMA((2, 3, count)),
            pltpu.SemaphoreType.DMA((4, count)),
            pltpu.SemaphoreType.DMA((4, count)),
        ],
        compiler_params=pltpu.CompilerParams(collective_id=0, has_side_effects=True),
        name="gather_tokens",
    )(moe_in, grad_out, table, key_value)


def reduce_kernel(
    part_ref,
    total_ref,
    beside_half,
    above_half,
    beside_full,
    above_full,
    to_beside,
    to_above,
    to_line,
    from_line,
    send_sem,
    recv_sem,
):
    seq = lax.axis_index("seq")
    count = lax.axis_size("seq")
    half = beside_half.shape[1]
    head, beside, above, corner = head_neighbours()
    greet((-1, 1), (beside, above))

    def pair(kind, source, target, p, peer):
        return send(source, target, send_sem.at[kind, p], recv_sem.at[kind, p], peer)

    def first(p):
        return (
            pair(
                0,
                part_ref.at[corner, p, pl.ds(0, half), :],
                beside_half.at[p],
                p,
                {"head": beside},
            ),
            pair(
                1,
                part_ref.at[corner, p, pl.ds(half, part_ref.shape[2] - half), :],
                above_half.at[p],
                p,
                {"head": above},
            ),
        )

    def second(p):
        return (
            pair(2, to_beside.at[p], beside_full.at[p], p, {"head": beside}),
            pair(3, to_above.at[p], above_full.at[p], p, {"head": above}),
        )

    def line(way, p, to):
        return pair(4 + way, to_line.at[p], from_line.at[way, p], p, {"seq": to})

    def at(k, body):
        for way, step in ((0, 1), (1, -1)):
            if k > 0 or way == 0:
                p = seq + step * k
                pl.when(inside(p, count))(lambda way=way, step=step, p=p: body(k, way, step, p))

    def start_first(k, way, step, p):
        for copy in first(p):
            copy.start()

    def add_first(k, way, step, p):
        from_beside, from_above = first(p)
        via_beside, via_above = second(p)
        from_beside.wait_recv()
        to_above[p, :half, :] = (
            part_ref[above, p, :half, :].astype(jnp.float32)
            + beside_half[p].astype(jnp.float32)
        ).astype(jnp.bfloat16)
        to_above[p, half:, :] = part_ref[above, p, half:, :]
        via_above.start()
        from_above.wait_recv()
        to_beside[p, :half, :] = part_ref[beside, p, :half, :]
        to_beside[p, half:, :] = (
            part_ref[beside, p, half:, :].astype(jnp.float32) + above_half[p].astype(jnp.float32)
        ).astype(jnp.bfloat16)
        via_beside.start()

    def add_second(k, way, step, p):
        for copy in second(p):
            copy.wait_recv()
        summed = (
            part_ref[head, p].astype(jnp.float32)
            + beside_full[p].astype(jnp.float32)
            + above_full[p].astype(jnp.float32)
        )
        if k > 0:
            to_line[p] = summed.astype(jnp.bfloat16)

            @pl.when(inside(seq - step, count))
            def _():
                line(way, p, seq - step).wait_recv()
                to_line[p] = (summed + from_line[way, p].astype(jnp.float32)).astype(jnp.bfloat16)

            line(way, p, seq + step).start()
        else:
            for other in range(count):

                @pl.when(seq == other)
                def _():
                    result = summed
                    if other > 0:
                        line(0, p, seq - 1).wait_recv()
                        result = result + from_line[0, p].astype(jnp.float32)
                    if other < count - 1:
                        line(1, p, seq + 1).wait_recv()
                        result = result + from_line[1, p].astype(jnp.float32)
                    total_ref[...] = result.astype(jnp.bfloat16)

    def finish(k, way, step, p):
        for copy in first(p) + second(p):
            copy.wait_send()
        if k > 0:
            line(way, p, seq + step).wait_send()

    for turn in range(count + 3):
        for body, behind in ((add_first, 2), (add_second, 3), (start_first, 0)):
            k = count - 1 - (turn - behind)
            if 0 <= k < count:
                at(k, body)
    for k in range(count):
        at(k, finish)


def reduce_tokens(part):
    _, count, rows, quarter = part.shape
    half = (rows - 16) // 2
    block = lambda *lead: pltpu.VMEM(lead + (rows, quarter), jnp.bfloat16)
    return pl.pallas_call(
        reduce_kernel,
        in_specs=[pl.BlockSpec(memory_space=pltpu.VMEM)],
        out_specs=pl.BlockSpec(memory_space=pltpu.VMEM),
        out_shape=jax.ShapeDtypeStruct((rows, quarter), jnp.bfloat16),
        scratch_shapes=[
            pltpu.VMEM((count, half, quarter), jnp.bfloat16),
            pltpu.VMEM((count, rows - half, quarter), jnp.bfloat16),
            block(count),
            block(count),
            block(count),
            block(count),
            block(count),
            block(2, count),
            pltpu.SemaphoreType.DMA((6, count)),
            pltpu.SemaphoreType.DMA((6, count)),
        ],
        compiler_params=pltpu.CompilerParams(collective_id=1, has_side_effects=True),
        name="reduce_tokens",
    )(part)


def attend_kernel(
    grad_ref,
    summed_ref,
    query_ref,
    window_ref,
    d_query_ref,
    total_ref,
    part_ref,
    landed,
    send_sem,
    recv_sem,
):
    seq = lax.axis_index("seq")
    count, shard, width = window_ref.shape
    head_dim = width // 2
    per_group = query_ref.shape[1] // head_dim
    scale = head_dim ** (-0.5)
    barrier = pltpu.get_barrier_semaphore()
    for offset in range(1, count):
        pl.semaphore_signal(
            barrier, inc=1, device_id={"seq": (seq + offset) % count}, device_id_type=MESH
        )
    window = jnp.concatenate([window_ref[p] for p in range(count)], axis=0)
    key_rows = window[:, :head_dim]
    value_rows = window[:, head_dim:]
    d_hidden = (
        grad_ref[...].astype(jnp.float32) + summed_ref[:shard, :].astype(jnp.float32)
    ).astype(jnp.bfloat16)
    position = seq * shard + lax.broadcasted_iota(jnp.int32, (shard, count * shard), 0)
    key_pos = lax.broadcasted_iota(jnp.int32, (shard, count * shard), 1)
    visible = (key_pos <= position) & (key_pos > position - WIN)
    d_keys = jnp.zeros((head_dim, count * shard), jnp.float32)
    d_values = jnp.zeros((head_dim, count * shard), jnp.float32)
    d_query = []
    for g in range(per_group):
        columns = slice(g * head_dim, (g + 1) * head_dim)
        query = query_ref[:, columns]
        grad = d_hidden[:, columns]
        scores = dot(query, key_rows, ((1,), (1,))) * scale
        scores = jnp.where(visible, scores, -1e30)
        raised = jnp.exp(scores - jnp.max(scores, axis=1, keepdims=True))
        probs = raised / jnp.sum(raised, axis=1, keepdims=True)
        d_probs = dot(grad, value_rows, ((1,), (1,)))
        row_dot = jnp.sum(probs * d_probs, axis=1, keepdims=True)
        d_scores = (probs * (d_probs - row_dot) * scale).astype(jnp.bfloat16)
        d_query.append(dot(d_scores, key_rows, ((1,), (0,))).astype(jnp.bfloat16))
        d_keys = d_keys + dot(query, d_scores, ((0,), (0,)))
        d_values = d_values + dot(grad, probs.astype(jnp.bfloat16), ((0,), (0,)))
    d_window = jnp.concatenate([d_keys, d_values], axis=0).T.astype(jnp.bfloat16)
    for p in range(count):
        part_ref[p] = d_window[p * shard : (p + 1) * shard]
    pl.semaphore_wait(barrier, count - 1)
    copies = []
    for offset in range(1, count):
        to = (seq + offset) % count
        copies.append(
            send(
                part_ref.at[to],
                landed.at[offset],
                send_sem.at[offset],
                recv_sem.at[offset],
                {"seq": to},
            )
        )
        copies[-1].start()
    d_query_ref[...] = jnp.concatenate(d_query, axis=1)
    summed = part_ref[seq].astype(jnp.float32)
    for offset, copy in enumerate(copies, 1):
        copy.wait_recv()
        summed = summed + landed[offset].astype(jnp.float32)
    total_ref[...] = summed.astype(jnp.bfloat16)
    for copy in copies:
        copy.wait_send()


def attend_and_return(grad_out, summed, queries, window):
    count, shard, width = window.shape
    return pl.pallas_call(
        attend_kernel,
        in_specs=[pl.BlockSpec(memory_space=pltpu.VMEM)] * 4,
        out_specs=[pl.BlockSpec(memory_space=pltpu.VMEM)] * 2,
        out_shape=[
            jax.ShapeDtypeStruct(queries.shape, jnp.bfloat16),
            jax.ShapeDtypeStruct((shard, width), jnp.bfloat16),
        ],
        scratch_shapes=[
            pltpu.VMEM(window.shape, jnp.bfloat16),
            pltpu.VMEM(window.shape, jnp.bfloat16),
            pltpu.SemaphoreType.DMA((count,)),
            pltpu.SemaphoreType.DMA((count,)),
        ],
        compiler_params=pltpu.CompilerParams(collective_id=2, has_side_effects=True),
        name="attend_and_return",
    )(grad_out, summed, queries, window)


def gathered_layer(moe_in, grad_out, routes, route_weight, w_gate, w_up, w_down, queries, key_value):
    shard, top = routes.shape
    table = jnp.concatenate(
        [routes.astype(jnp.float32).T, route_weight.astype(jnp.float32).T], axis=0
    )
    own_rows = key_value.reshape(shard, key_value.shape[2])
    tokens, tables, window = gather_tokens(moe_in, grad_out, table, own_rows)
    grad_gate, grad_up, grad_down, d_moe = run_experts(tables, tokens, w_gate, w_up, w_down)
    summed = reduce_tokens(d_moe)
    d_moe_in = summed[:shard]
    d_route_weight = summed[shard : shard + top, :shard].T
    d_queries, d_own = attend_and_return(grad_out, summed, queries, window)
    d_key_value = d_own.reshape(key_value.shape)
    return (d_moe_in, d_route_weight, grad_gate, grad_up, grad_down, d_queries, d_key_value)


def shards(moe_in, grad_out, routes, route_weight, w_gate, w_up, w_down, queries, key_value):
    gathered_rows = lax.axis_size("seq") * moe_in.shape[0]
    if gathered_rows <= EXPERTS * CAP and lax.axis_size("head") == 4:
        return gathered_layer(
            moe_in, grad_out, routes, route_weight, w_gate, w_up, w_down, queries, key_value
        )
    d_moe_in, d_route_weight, grad_gate, grad_up, grad_down = dispatched_experts(
        moe_in, grad_out, routes, route_weight, w_gate, w_up, w_down
    )
    d_queries, d_key_value = attention(grad_out, d_moe_in, queries, key_value)
    return (d_moe_in, d_route_weight, grad_gate, grad_up, grad_down, d_queries, d_key_value)


def solution(mesh):
    in_specs = (
        P(("rep", "seq"), "head"),
        P(("rep", "seq"), "head"),
        P(("rep", "seq"), None),
        P(("rep", "seq"), None),
        P("seq", None, "head"),
        P("seq", None, "head"),
        P("seq", "head", None),
        P(("rep", "seq"), "head"),
        P(("rep", "seq"), "head", None),
    )
    out_specs = (
        P(("rep", "seq"), "head"),
        P(("rep", "seq"), None),
        P(("rep", "seq"), None, "head"),
        P(("rep", "seq"), None, "head"),
        P(("rep", "seq"), "head", None),
        P(("rep", "seq"), "head"),
        P(("rep", "seq"), "head", None),
    )
    return jax.shard_map(shards, mesh=mesh, in_specs=in_specs, out_specs=out_specs, check_vma=False)
```

```python
import jax
import jax.numpy as jnp
from jax import lax
from jax.experimental import pallas as pl
from jax.experimental.pallas import tpu as pltpu
from jax.sharding import PartitionSpec as P

EXPERTS = 64
WIN = 512
CAP = 18
MESH = pl.DeviceIdType.MESH


def shifted(block, axis, distance):
    devices = range(lax.axis_size(axis))
    route = [(i - distance, i) for i in devices if i - distance in devices]
    return lax.ppermute(block, axis, route)


def slot_tables(routes, route_weight):
    token_rows, top_count = routes.shape
    flat_expert = routes.reshape(token_rows * top_count)
    expert_ids = jnp.arange(EXPERTS, dtype=jnp.int32)
    one_hot = (flat_expert[:, None] == expert_ids[None, :]).astype(jnp.int32)
    earlier = jnp.cumsum(one_hot, axis=0) - one_hot
    slot_rank = jnp.sum(earlier * one_hot, axis=1)
    target = flat_expert * CAP + slot_rank
    slot_cells = jnp.arange(EXPERTS * CAP, dtype=jnp.int32)
    chosen = (target[None, :] == slot_cells[:, None]).astype(jnp.float32)
    by_token = jnp.sum(chosen.reshape(EXPERTS * CAP, token_rows, top_count), axis=2).astype(
        jnp.bfloat16
    )
    slot_weight = jnp.dot(
        chosen,
        route_weight.reshape(token_rows * top_count).astype(jnp.float32),
        precision=lax.Precision.HIGHEST,
    )
    return (chosen, by_token, slot_weight.astype(jnp.bfloat16).reshape(EXPERTS, CAP))


def place_rows(by_token, source):
    placed = jnp.dot(by_token, source, preferred_element_type=jnp.float32)
    return placed.astype(jnp.bfloat16).reshape(EXPERTS, CAP, source.shape[1])


def fetch_window(own_rows, reach):
    earlier_shards = [shifted(own_rows, "seq", offset) for offset in range(reach, 0, -1)]
    window = jnp.concatenate(earlier_shards + [own_rows], axis=0)
    return window


def return_window(d_window, reach, shard):
    summed = d_window[reach * shard :]
    for offset in range(1, reach + 1):
        begin = (reach - offset) * shard
        summed = summed + shifted(
            d_window[begin : begin + shard].astype(jnp.bfloat16), "seq", -offset
        ).astype(jnp.float32)
    return summed


def dispatched_experts(moe_in, grad_out, routes, route_weight, w_gate, w_up, w_down):
    seq_count = lax.axis_size("seq")
    local_experts = w_gate.shape[0]
    chosen, by_token, slot_weight = slot_tables(routes, route_weight)
    part_in, part_grad, got_weight = (
        lax.all_to_all(
            place_rows(by_token, moe_in), "seq", split_axis=0, concat_axis=0, tiled=True
        ),
        lax.all_to_all(
            place_rows(by_token, grad_out), "seq", split_axis=0, concat_axis=0, tiled=True
        ),
        lax.all_to_all(slot_weight, "seq", split_axis=0, concat_axis=0, tiled=True),
    )
    got_in, got_grad = (
        lax.all_gather(part_in, "head", axis=2, tiled=True),
        lax.all_gather(part_grad, "head", axis=2, tiled=True),
    )
    width = got_in.shape[2]
    rows_in = got_in.reshape(seq_count, local_experts, CAP, width)
    rows_grad = got_grad.reshape(seq_count, local_experts, CAP, width)
    scale_w = got_weight.reshape(seq_count, local_experts, CAP).astype(jnp.float32)[..., None]
    gate_pre = jnp.einsum("secd,edf->secf", rows_in, w_gate, preferred_element_type=jnp.float32)
    up_pre = jnp.einsum("secd,edf->secf", rows_in, w_up, preferred_element_type=jnp.float32)
    back_proj = jnp.einsum("secd,efd->secf", rows_grad, w_down, preferred_element_type=jnp.float32)
    sigmoid_gate = jax.nn.sigmoid(gate_pre)
    silu_gate = gate_pre * sigmoid_gate
    active = silu_gate * up_pre
    route_part = jnp.sum(active * back_proj, axis=3)
    d_active = scale_w * back_proj
    d_gate = (d_active * up_pre * sigmoid_gate * (1.0 + gate_pre * (1.0 - sigmoid_gate))).astype(
        jnp.bfloat16
    )
    d_up = (d_active * silu_gate).astype(jnp.bfloat16)
    weighted = (scale_w * active).astype(jnp.bfloat16)
    rows_back = jnp.einsum("secf,edf->secd", d_gate, w_gate, preferred_element_type=jnp.float32)
    rows_back = rows_back + jnp.einsum(
        "secf,edf->secd", d_up, w_up, preferred_element_type=jnp.float32
    )
    rows_quarter = lax.psum_scatter(
        rows_back.reshape(seq_count * local_experts, CAP, width).astype(jnp.bfloat16),
        "head",
        scatter_dimension=2,
        tiled=True,
    )
    route_sum = lax.psum(route_part, "head").astype(jnp.bfloat16)
    grad_gate = jnp.einsum(
        "secd,secf->edf", rows_in, d_gate, preferred_element_type=jnp.float32
    ).astype(jnp.bfloat16)
    grad_up = jnp.einsum(
        "secd,secf->edf", rows_in, d_up, preferred_element_type=jnp.float32
    ).astype(jnp.bfloat16)
    grad_down = jnp.einsum(
        "secf,secd->efd", weighted, rows_grad, preferred_element_type=jnp.float32
    ).astype(jnp.bfloat16)
    back_rows, back_weight = (
        lax.all_to_all(rows_quarter, "seq", split_axis=0, concat_axis=0, tiled=True),
        lax.all_to_all(
            route_sum.reshape(seq_count * local_experts, CAP),
            "seq",
            split_axis=0,
            concat_axis=0,
            tiled=True,
        ),
    )
    quarter = back_rows.shape[2]
    d_moe_in = jnp.einsum(
        "st,sd->td",
        by_token,
        back_rows.reshape(EXPERTS * CAP, quarter),
        preferred_element_type=jnp.float32,
    ).astype(jnp.bfloat16)
    d_route = jnp.dot(
        back_weight.reshape(EXPERTS * CAP).astype(jnp.float32),
        chosen,
        precision=lax.Precision.HIGHEST,
    )
    d_route_weight = d_route.astype(jnp.bfloat16).reshape(routes.shape)
    return (d_moe_in, d_route_weight, grad_gate, grad_up, grad_down)


def attend(grad_out, d_moe_in, queries, window, first_shard):
    tokens = grad_out.shape[0]
    head_dim = window.shape[1] // 2
    per_group = queries.shape[1] // head_dim
    scale = head_dim ** (-0.5)
    d_hidden = (grad_out.astype(jnp.float32) + d_moe_in.astype(jnp.float32)).astype(jnp.bfloat16)
    query_rows = queries.reshape(tokens * per_group, head_dim)
    grad_rows = d_hidden.reshape(tokens * per_group, head_dim)
    key_rows = window[:, :head_dim]
    value_rows = window[:, head_dim:]
    contract_last = (((1,), (1,)), ((), ()))
    contract_first = (((0,), (0,)), ((), ()))
    seq_index = lax.axis_index("seq")
    key_pos = first_shard * tokens + jnp.arange(window.shape[0], dtype=jnp.int32)
    row_total = tokens * per_group
    block_rows = min(512, row_total)
    block_count = row_total // block_rows

    def attend_block(index, carry):
        d_window, d_query_all = carry
        begin = (index * block_rows).astype(jnp.int32)
        query_blk = lax.dynamic_slice_in_dim(query_rows, begin, block_rows, 0)
        grad_blk = lax.dynamic_slice_in_dim(grad_rows, begin, block_rows, 0)
        scores = (
            lax.dot_general(query_blk, key_rows, contract_last, preferred_element_type=jnp.float32)
            * scale
        )
        position = (
            seq_index * tokens + (begin + jnp.arange(block_rows, dtype=jnp.int32)) // per_group
        )
        visible = (
            (key_pos[None, :] >= 0)
            & (key_pos[None, :] <= position[:, None])
            & (key_pos[None, :] > position[:, None] - WIN)
        )
        scores = jnp.where(visible, scores, -1e30)
        row_max = jnp.max(scores, axis=1, keepdims=True)
        raised = jnp.exp(scores - row_max)
        probs = raised / jnp.sum(raised, axis=1, keepdims=True)
        d_probs = lax.dot_general(
            grad_blk, value_rows, contract_last, preferred_element_type=jnp.float32
        )
        row_dot = jnp.sum(probs * d_probs, axis=1, keepdims=True)
        d_scores = (probs * (d_probs - row_dot) * scale).astype(jnp.bfloat16)
        probs_low = probs.astype(jnp.bfloat16)
        d_query_blk = jnp.dot(d_scores, key_rows, preferred_element_type=jnp.float32).astype(
            jnp.bfloat16
        )
        d_keys = lax.dot_general(
            d_scores, query_blk, contract_first, preferred_element_type=jnp.float32
        )
        d_values = lax.dot_general(
            probs_low, grad_blk, contract_first, preferred_element_type=jnp.float32
        )
        d_window = d_window + jnp.concatenate([d_keys, d_values], axis=1)
        d_query_all = lax.dynamic_update_slice_in_dim(d_query_all, d_query_blk, begin, 0)
        return (d_window, d_query_all)

    window_start = jnp.zeros(window.shape, jnp.float32)
    query_start = jnp.zeros((row_total, head_dim), jnp.bfloat16)
    d_window, d_query_all = lax.fori_loop(0, block_count, attend_block, (window_start, query_start))
    d_queries = d_query_all.reshape(tokens, per_group * head_dim)
    return (d_queries, d_window)


def attention(grad_out, d_moe_in, queries, key_value):
    tokens = grad_out.shape[0]
    reach = min(WIN // tokens, lax.axis_size("seq") - 1)
    window = fetch_window(key_value.reshape(tokens, key_value.shape[2]), reach)
    first_shard = lax.axis_index("seq") - reach
    d_queries, d_window = attend(grad_out, d_moe_in, queries, window, first_shard)
    d_own = return_window(d_window, reach, tokens)
    d_key_value = d_own.astype(jnp.bfloat16).reshape(key_value.shape)
    return (d_queries, d_key_value)


def dot(a, b, contract):
    return lax.dot_general(a, b, (contract, ((), ())), preferred_element_type=jnp.float32)


def expert_kernel(
    tables_ref,
    tokens_ref,
    wg_ref,
    wu_ref,
    wd_ref,
    gg_ref,
    gu_ref,
    gd_ref,
    dmoe_ref,
    routes_ref,
    weight_ref,
    droute_ref,
    rank_ref,
    dense_ref,
    pick_ref,
    back_ref,
):
    group = pl.program_id(0)
    per_step = wg_ref.shape[0]
    _, heads, total, quarter = tokens_ref.shape
    shard_count, double_top, shard = tables_ref.shape
    top = double_top // 2
    hidden = wg_ref.shape[2]
    rows = pick_ref.shape[0] // rank_ref.shape[0]
    local = rank_ref.shape[0]

    @pl.when(group == 0)
    def _():
        first = (lax.axis_index("seq") * local).astype(jnp.float32)
        for s in range(shard_count):
            columns = slice(s * shard, (s + 1) * shard)
            routes_ref[:, columns] = tables_ref[s, :top, :] - first
            weight_ref[:, columns] = tables_ref[s, top:, :]
        for index in range(local):
            hit = routes_ref[...] == index
            named = jnp.sum(hit.astype(jnp.float32), axis=0, keepdims=True)
            rank_ref[pl.ds(index, 1), :] = named
            dense_ref[pl.ds(index, 1), :] = jnp.sum(
                jnp.where(hit, weight_ref[...], 0.0), axis=0, keepdims=True
            )
        named = rank_ref[...]
        before = lax.broadcasted_iota(jnp.int32, (total, total), 0)
        after = lax.broadcasted_iota(jnp.int32, (total, total), 1)
        order = (before < after).astype(jnp.float32).astype(jnp.bfloat16)
        earlier = dot(named.astype(jnp.bfloat16), order, ((1,), (0,)))
        rank_ref[...] = jnp.where(named > 0.5, earlier, -1.0)
        droute_ref[...] = jnp.zeros_like(droute_ref)

    slots = lax.broadcasted_iota(jnp.int32, (rows, total), 0).astype(jnp.float32)

    def choose(j):
        expert = group * per_step + j
        chosen = rank_ref[pl.ds(expert, 1), :] == slots
        pick = chosen.astype(jnp.float32).astype(jnp.bfloat16)
        scale_w = jnp.sum(
            jnp.where(chosen, dense_ref[pl.ds(expert, 1), :], 0.0), axis=1, keepdims=True
        )
        return expert, chosen, pick, scale_w

    choices = [choose(j) for j in range(per_step)]
    picks = jnp.concatenate([pick for _, _, pick, _ in choices], axis=0)
    x_all, dy_all = (
        jnp.concatenate(
            [
                dot(picks, tokens_ref[part, h], ((1,), (0,))).astype(jnp.bfloat16)
                for h in range(heads)
            ],
            axis=1,
        )
        for part in range(2)
    )
    start = pl.multiple_of(group * (per_step * rows), rows)
    pick_ref[pl.ds(start, per_step * rows), :] = picks
    forward = []
    for j, (expert, chosen, _, scale_w) in enumerate(choices):
        x = x_all[j * rows : (j + 1) * rows]
        dy = dy_all[j * rows : (j + 1) * rows]
        w_both = jnp.concatenate([wg_ref[j], wu_ref[j]], axis=1)
        pre = dot(x, w_both, ((1,), (0,)))
        back_proj = dot(dy, wd_ref[j], ((1,), (1,)))
        forward.append((x, dy, w_both, pre, back_proj))
    backward = []
    for (expert, chosen, _, scale_w), (x, dy, w_both, pre, back_proj) in zip(choices, forward):
        gate_pre = pre[:, :hidden]
        up_pre = pre[:, hidden:]
        sigmoid_gate = jax.nn.sigmoid(gate_pre)
        silu_gate = gate_pre * sigmoid_gate
        active = silu_gate * up_pre
        route_part = jnp.sum(active * back_proj, axis=1, keepdims=True)
        route_row = jnp.sum(jnp.where(chosen, route_part, 0.0), axis=0, keepdims=True)
        droute_ref[...] += jnp.where(
            routes_ref[...] == expert.astype(jnp.float32), route_row, 0.0
        )
        d_active = scale_w * back_proj
        d_gate = d_active * up_pre * sigmoid_gate * (1.0 + gate_pre * (1.0 - sigmoid_gate))
        d_up = d_active * silu_gate
        d_both = jnp.concatenate([d_gate, d_up], axis=1).astype(jnp.bfloat16)
        backward.append((d_both, (scale_w * active).astype(jnp.bfloat16)))
    for j, (x, dy, w_both, _, _) in enumerate(forward):
        d_both, weighted = backward[j]
        back_ref[pl.ds(start + j * rows, rows), :] = dot(d_both, w_both, ((1,), (1,))).astype(
            jnp.bfloat16
        )
        grad_both = dot(x, d_both, ((0,), (0,))).astype(jnp.bfloat16)
        gg_ref[j] = grad_both[:, :hidden]
        gu_ref[j] = grad_both[:, hidden:]
        gd_ref[j] = dot(weighted, dy, ((0,), (0,))).astype(jnp.bfloat16)

    @pl.when(group == pl.num_programs(0) - 1)
    def _():
        for h in range(heads):
            columns = slice(h * quarter, (h + 1) * quarter)
            summed = dot(pick_ref[...], back_ref[:, columns], ((0,), (0,))).astype(jnp.bfloat16)
            for s in range(shard_count):
                dmoe_ref[h, s, :shard, :] = summed[s * shard : (s + 1) * shard]
                share = droute_ref[:, s * shard : (s + 1) * shard]
                share = jnp.concatenate([share, jnp.zeros((16 - top, shard), jnp.float32)], axis=0)
                if quarter > shard:
                    blank = jnp.zeros((16, quarter - shard), jnp.float32)
                    share = jnp.concatenate([share, blank], axis=1)
                dmoe_ref[h, s, shard:, :] = share.astype(jnp.bfloat16)


def run_experts(tables, tokens, w_gate, w_up, w_down):
    local, width, hidden = w_gate.shape
    _, heads, total, quarter = tokens.shape
    shard_count, double_top, shard = tables.shape
    top = double_top // 2
    rows = -(-shard_count * CAP // 16) * 16
    whole = lambda *shape: pl.BlockSpec(shape, lambda e: (0,) * len(shape))
    per_step = 2 if local % 2 == 0 else 1
    wide = pl.BlockSpec((per_step, width, hidden), lambda e: (e, 0, 0))
    tall = pl.BlockSpec((per_step, hidden, width), lambda e: (e, 0, 0))
    back_shape = (heads, shard_count, shard + 16, quarter)
    return pl.pallas_call(
        expert_kernel,
        grid=(local // per_step,),
        in_specs=[whole(*tables.shape), whole(*tokens.shape), wide, wide, tall],
        out_specs=[wide, wide, tall, whole(*back_shape)],
        out_shape=[
            jax.ShapeDtypeStruct(w_gate.shape, jnp.bfloat16),
            jax.ShapeDtypeStruct(w_up.shape, jnp.bfloat16),
            jax.ShapeDtypeStruct(w_down.shape, jnp.bfloat16),
            jax.ShapeDtypeStruct(back_shape, jnp.bfloat16),
        ],
        scratch_shapes=[
            pltpu.VMEM((top, total), jnp.float32),
            pltpu.VMEM((top, total), jnp.float32),
            pltpu.VMEM((top, total), jnp.float32),
            pltpu.VMEM((local, total), jnp.float32),
            pltpu.VMEM((local, total), jnp.float32),
            pltpu.VMEM((local * rows, total), jnp.bfloat16),
            pltpu.VMEM((local * rows, width), jnp.bfloat16),
        ],
        compiler_params=pltpu.CompilerParams(vmem_limit_bytes=60 << 20),
        name="experts",
    )(tables, tokens, w_gate, w_up, w_down)


def head_neighbours():
    head = lax.axis_index("head")
    return head, head + 1 - 2 * (head % 2), (head + 2) % 4, (head + 3 - 2 * (head % 2)) % 4


def inside(index, count):
    return (index >= 0) & (index < count)


def greet(along, across):
    seq = lax.axis_index("seq")
    count = lax.axis_size("seq")
    barrier = pltpu.get_barrier_semaphore()
    for peer in across:
        pl.semaphore_signal(barrier, inc=1, device_id={"head": peer}, device_id_type=MESH)
    for step in along:

        @pl.when(inside(seq + step, count))
        def _():
            pl.semaphore_signal(
                barrier, inc=1, device_id={"seq": seq + step}, device_id_type=MESH
            )

    ends = (seq == 0).astype(jnp.int32) + (seq == count - 1).astype(jnp.int32)
    pl.semaphore_wait(barrier, len(across) + len(along) - ends)


def send(source, target, send_sem, recv_sem, peer):
    return pltpu.make_async_remote_copy(
        src_ref=source,
        dst_ref=target,
        send_sem=send_sem,
        recv_sem=recv_sem,
        device_id=peer,
        device_id_type=MESH,
    )


def gather_kernel(
    in_ref,
    grad_ref,
    routes_ref,
    weight_ref,
    kv_ref,
    tokens_ref,
    tables_ref,
    window_ref,
    own_sem,
    line_send,
    line_recv,
    square_send,
    square_recv,
):
    seq = lax.axis_index("seq")
    count = lax.axis_size("seq")
    shard = in_ref.shape[0]
    half = shard // 2
    head, beside, above, corner = head_neighbours()

    def piece(of, p):
        return tokens_ref.at[:, of, pl.ds(p * shard, shard), :]

    def upper(of, p):
        return tokens_ref.at[:, of, pl.ds(p * shard, half), :]

    def lower(of, p):
        return tokens_ref.at[:, of, pl.ds(p * shard + half, half), :]

    own_rows = pl.ds(seq * shard, shard)
    own = [
        pltpu.make_async_copy(in_ref, tokens_ref.at[0, head, own_rows, :], own_sem.at[0]),
        pltpu.make_async_copy(grad_ref, tokens_ref.at[1, head, own_rows, :], own_sem.at[1]),
        pltpu.make_async_copy(kv_ref, window_ref.at[seq], own_sem.at[2]),
    ]
    for copy in own:
        copy.start()
    tables_ref[seq] = jnp.concatenate(
        [routes_ref[...].astype(jnp.float32), weight_ref[...].astype(jnp.float32)], axis=0
    )
    greet((-1, 1), (beside, above))
    for copy in own:
        copy.wait()

    def line(way, p, to):
        refs = (piece(head, p), tables_ref.at[p], window_ref.at[p])
        return [
            send(ref, ref, line_send.at[way, j, p], line_recv.at[way, j, p], {"seq": to})
            for j, ref in enumerate(refs)
        ]

    def square(kind, ref, p, to):
        return send(ref, ref, square_send.at[kind, p], square_recv.at[kind, p], {"head": to})

    def forward(p):
        square(0, piece(beside, p), p, beside).wait_recv()
        square(2, upper(beside, p), p, above).start()
        square(1, piece(above, p), p, above).wait_recv()
        square(3, lower(above, p), p, beside).start()

    ways = ((0, 1), (1, -1))
    for k in range(count):
        if k == 1:
            forward(seq)
        for way, step in ways:
            p = seq - step * k

            @pl.when(inside(p, count))
            def _():
                if k > 0:
                    for copy in line(way, p, seq - step):
                        copy.wait_recv()

                @pl.when(inside(seq + step, count))
                def _():
                    for copy in line(way, p, seq + step):
                        copy.start()

                if k > 0 or way == 0:
                    square(0, piece(head, p), p, beside).start()
                    square(1, piece(head, p), p, above).start()

        if k > 1:
            for way, step in ways:
                if k > 1 or way == 0:
                    p = seq - step * (k - 1)
                    pl.when(inside(p, count))(lambda p=p: forward(p))
    for way, step in ways:
        if count > 1 or way == 0:
            p = seq - step * (count - 1)
            pl.when(inside(p, count))(lambda p=p: forward(p))
    for p in range(count):
        square(2, upper(corner, p), p, above).wait_recv()
        square(3, lower(corner, p), p, beside).wait_recv()
        square(0, piece(head, p), p, beside).wait_send()
        square(1, piece(head, p), p, above).wait_send()
        square(2, upper(beside, p), p, above).wait_send()
        square(3, lower(above, p), p, beside).wait_send()
    for k in range(count):
        for way, step in ways:
            p = seq - step * k

            @pl.when(inside(p, count) & inside(seq + step, count))
            def _():
                for copy in line(way, p, seq + step):
                    copy.wait_send()


def gather_tokens(moe_in, grad_out, routes_t, weight_t, key_value):
    heads = lax.axis_size("head")
    count = lax.axis_size("seq")
    shard, quarter = moe_in.shape
    return pl.pallas_call(
        gather_kernel,
        in_specs=[pl.BlockSpec(memory_space=pltpu.VMEM)] * 5,
        out_specs=[pl.BlockSpec(memory_space=pltpu.VMEM)] * 3,
        out_shape=[
            jax.ShapeDtypeStruct((2, heads, count * shard, quarter), jnp.bfloat16),
            jax.ShapeDtypeStruct((count, 2 * routes_t.shape[0], shard), jnp.float32),
            jax.ShapeDtypeStruct((count,) + key_value.shape, jnp.bfloat16),
        ],
        scratch_shapes=[
            pltpu.SemaphoreType.DMA((3,)),
            pltpu.SemaphoreType.DMA((2, 3, count)),
            pltpu.SemaphoreType.DMA((2, 3, count)),
            pltpu.SemaphoreType.DMA((4, count)),
            pltpu.SemaphoreType.DMA((4, count)),
        ],
        compiler_params=pltpu.CompilerParams(collective_id=0, has_side_effects=True),
        name="gather_tokens",
    )(moe_in, grad_out, routes_t, weight_t, key_value)


def reduce_kernel(
    part_ref,
    total_ref,
    beside_half,
    above_half,
    beside_full,
    above_full,
    to_beside,
    to_above,
    to_line,
    from_line,
    send_sem,
    recv_sem,
):
    seq = lax.axis_index("seq")
    count = lax.axis_size("seq")
    half = beside_half.shape[1]
    head, beside, above, corner = head_neighbours()
    greet((-1, 1), (beside, above))

    def pair(kind, source, target, p, peer):
        return send(source, target, send_sem.at[kind, p], recv_sem.at[kind, p], peer)

    def first(p):
        return (
            pair(
                0,
                part_ref.at[corner, p, pl.ds(0, half), :],
                beside_half.at[p],
                p,
                {"head": beside},
            ),
            pair(
                1,
                part_ref.at[corner, p, pl.ds(half, part_ref.shape[2] - half), :],
                above_half.at[p],
                p,
                {"head": above},
            ),
        )

    def second(p):
        return (
            pair(2, to_beside.at[p], beside_full.at[p], p, {"head": beside}),
            pair(3, to_above.at[p], above_full.at[p], p, {"head": above}),
        )

    def line(way, p, to):
        return pair(4 + way, to_line.at[p], from_line.at[way, p], p, {"seq": to})

    def at(k, body):
        for way, step in ((0, 1), (1, -1)):
            if k > 0 or way == 0:
                p = seq + step * k
                pl.when(inside(p, count))(lambda way=way, step=step, p=p: body(k, way, step, p))

    def start_first(k, way, step, p):
        for copy in first(p):
            copy.start()

    def add_first(k, way, step, p):
        from_beside, from_above = first(p)
        via_beside, via_above = second(p)
        from_beside.wait_recv()
        to_above[p, :half, :] = (
            part_ref[above, p, :half, :].astype(jnp.float32)
            + beside_half[p].astype(jnp.float32)
        ).astype(jnp.bfloat16)
        to_above[p, half:, :] = part_ref[above, p, half:, :]
        via_above.start()
        from_above.wait_recv()
        to_beside[p, :half, :] = part_ref[beside, p, :half, :]
        to_beside[p, half:, :] = (
            part_ref[beside, p, half:, :].astype(jnp.float32) + above_half[p].astype(jnp.float32)
        ).astype(jnp.bfloat16)
        via_beside.start()

    def add_second(k, way, step, p):
        for copy in second(p):
            copy.wait_recv()
        summed = (
            part_ref[head, p].astype(jnp.float32)
            + beside_full[p].astype(jnp.float32)
            + above_full[p].astype(jnp.float32)
        )
        if k > 0:
            to_line[p] = summed.astype(jnp.bfloat16)

            @pl.when(inside(seq - step, count))
            def _():
                line(way, p, seq - step).wait_recv()
                to_line[p] = (summed + from_line[way, p].astype(jnp.float32)).astype(jnp.bfloat16)

            line(way, p, seq + step).start()
        else:
            for other in range(count):

                @pl.when(seq == other)
                def _():
                    result = summed
                    if other > 0:
                        line(0, p, seq - 1).wait_recv()
                        result = result + from_line[0, p].astype(jnp.float32)
                    if other < count - 1:
                        line(1, p, seq + 1).wait_recv()
                        result = result + from_line[1, p].astype(jnp.float32)
                    total_ref[...] = result.astype(jnp.bfloat16)

    def finish(k, way, step, p):
        for copy in first(p) + second(p):
            copy.wait_send()
        if k > 0:
            line(way, p, seq + step).wait_send()

    for turn in range(count + 3):
        for body, behind in ((add_first, 2), (add_second, 3), (start_first, 0)):
            k = count - 1 - (turn - behind)
            if 0 <= k < count:
                at(k, body)
    for k in range(count):
        at(k, finish)


def reduce_tokens(part):
    _, count, rows, quarter = part.shape
    half = (rows - 16) // 2
    block = lambda *lead: pltpu.VMEM(lead + (rows, quarter), jnp.bfloat16)
    return pl.pallas_call(
        reduce_kernel,
        in_specs=[pl.BlockSpec(memory_space=pltpu.VMEM)],
        out_specs=pl.BlockSpec(memory_space=pltpu.VMEM),
        out_shape=jax.ShapeDtypeStruct((rows, quarter), jnp.bfloat16),
        scratch_shapes=[
            pltpu.VMEM((count, half, quarter), jnp.bfloat16),
            pltpu.VMEM((count, rows - half, quarter), jnp.bfloat16),
            block(count),
            block(count),
            block(count),
            block(count),
            block(count),
            block(2, count),
            pltpu.SemaphoreType.DMA((6, count)),
            pltpu.SemaphoreType.DMA((6, count)),
        ],
        compiler_params=pltpu.CompilerParams(collective_id=1, has_side_effects=True),
        name="reduce_tokens",
    )(part)


def attend_kernel(
    grad_ref,
    summed_ref,
    query_ref,
    window_ref,
    d_query_ref,
    total_ref,
    part_ref,
    landed,
    send_sem,
    recv_sem,
):
    seq = lax.axis_index("seq")
    count, shard, width = window_ref.shape
    head_dim = width // 2
    per_group = query_ref.shape[1] // head_dim
    scale = head_dim ** (-0.5)
    barrier = pltpu.get_barrier_semaphore()
    for offset in range(1, count):
        pl.semaphore_signal(
            barrier, inc=1, device_id={"seq": (seq + offset) % count}, device_id_type=MESH
        )
    window = jnp.concatenate([window_ref[p] for p in range(count)], axis=0)
    key_rows = window[:, :head_dim]
    value_rows = window[:, head_dim:]
    d_hidden = (
        grad_ref[...].astype(jnp.float32) + summed_ref[:shard, :].astype(jnp.float32)
    ).astype(jnp.bfloat16)
    position = seq * shard + lax.broadcasted_iota(jnp.int32, (shard, count * shard), 0)
    key_pos = lax.broadcasted_iota(jnp.int32, (shard, count * shard), 1)
    visible = (key_pos <= position) & (key_pos > position - WIN)
    d_keys = jnp.zeros((head_dim, count * shard), jnp.float32)
    d_values = jnp.zeros((head_dim, count * shard), jnp.float32)
    d_query = []
    for g in range(per_group):
        columns = slice(g * head_dim, (g + 1) * head_dim)
        query = query_ref[:, columns]
        grad = d_hidden[:, columns]
        scores = dot(query, key_rows, ((1,), (1,))) * scale
        scores = jnp.where(visible, scores, -1e30)
        raised = jnp.exp(scores - jnp.max(scores, axis=1, keepdims=True))
        probs = raised / jnp.sum(raised, axis=1, keepdims=True)
        d_probs = dot(grad, value_rows, ((1,), (1,)))
        row_dot = jnp.sum(probs * d_probs, axis=1, keepdims=True)
        d_scores = (probs * (d_probs - row_dot) * scale).astype(jnp.bfloat16)
        d_query.append(dot(d_scores, key_rows, ((1,), (0,))).astype(jnp.bfloat16))
        d_keys = d_keys + dot(query, d_scores, ((0,), (0,)))
        d_values = d_values + dot(grad, probs.astype(jnp.bfloat16), ((0,), (0,)))
    d_window = jnp.concatenate([d_keys, d_values], axis=0).T.astype(jnp.bfloat16)
    for p in range(count):
        part_ref[p] = d_window[p * shard : (p + 1) * shard]
    pl.semaphore_wait(barrier, count - 1)
    copies = []
    for offset in range(1, count):
        to = (seq + offset) % count
        copies.append(
            send(
                part_ref.at[to],
                landed.at[offset],
                send_sem.at[offset],
                recv_sem.at[offset],
                {"seq": to},
            )
        )
        copies[-1].start()
    d_query_ref[...] = jnp.concatenate(d_query, axis=1)
    summed = part_ref[seq].astype(jnp.float32)
    for offset, copy in enumerate(copies, 1):
        copy.wait_recv()
        summed = summed + landed[offset].astype(jnp.float32)
    total_ref[...] = summed.astype(jnp.bfloat16)
    for copy in copies:
        copy.wait_send()


def attend_and_return(grad_out, summed, queries, window):
    count, shard, width = window.shape
    return pl.pallas_call(
        attend_kernel,
        in_specs=[pl.BlockSpec(memory_space=pltpu.VMEM)] * 4,
        out_specs=[pl.BlockSpec(memory_space=pltpu.VMEM)] * 2,
        out_shape=[
            jax.ShapeDtypeStruct(queries.shape, jnp.bfloat16),
            jax.ShapeDtypeStruct((shard, width), jnp.bfloat16),
        ],
        scratch_shapes=[
            pltpu.VMEM(window.shape, jnp.bfloat16),
            pltpu.VMEM(window.shape, jnp.bfloat16),
            pltpu.SemaphoreType.DMA((count,)),
            pltpu.SemaphoreType.DMA((count,)),
        ],
        compiler_params=pltpu.CompilerParams(collective_id=2, has_side_effects=True),
        name="attend_and_return",
    )(grad_out, summed, queries, window)


def gathered_layer(moe_in, grad_out, routes, route_weight, w_gate, w_up, w_down, queries, key_value):
    shard, top = routes.shape
    own_rows = key_value.reshape(shard, key_value.shape[2])
    tokens, tables, window = gather_tokens(
        moe_in, grad_out, routes.T, route_weight.T, own_rows
    )
    grad_gate, grad_up, grad_down, d_moe = run_experts(tables, tokens, w_gate, w_up, w_down)
    summed = reduce_tokens(d_moe)
    d_moe_in = summed[:shard]
    d_route_weight = summed[shard : shard + top, :shard].T
    d_queries, d_own = attend_and_return(grad_out, summed, queries, window)
    d_key_value = d_own.reshape(key_value.shape)
    return (d_moe_in, d_route_weight, grad_gate, grad_up, grad_down, d_queries, d_key_value)


def shards(moe_in, grad_out, routes, route_weight, w_gate, w_up, w_down, queries, key_value):
    gathered_rows = lax.axis_size("seq") * moe_in.shape[0]
    if gathered_rows <= EXPERTS * CAP and lax.axis_size("head") == 4:
        return gathered_layer(
            moe_in, grad_out, routes, route_weight, w_gate, w_up, w_down, queries, key_value
        )
    d_moe_in, d_route_weight, grad_gate, grad_up, grad_down = dispatched_experts(
        moe_in, grad_out, routes, route_weight, w_gate, w_up, w_down
    )
    d_queries, d_key_value = attention(grad_out, d_moe_in, queries, key_value)
    return (d_moe_in, d_route_weight, grad_gate, grad_up, grad_down, d_queries, d_key_value)


def solution(mesh):
    in_specs = (
        P(("rep", "seq"), "head"),
        P(("rep", "seq"), "head"),
        P(("rep", "seq"), None),
        P(("rep", "seq"), None),
        P("seq", None, "head"),
        P("seq", None, "head"),
        P("seq", "head", None),
        P(("rep", "seq"), "head"),
        P(("rep", "seq"), "head", None),
    )
    out_specs = (
        P(("rep", "seq"), "head"),
        P(("rep", "seq"), None),
        P(("rep", "seq"), None, "head"),
        P(("rep", "seq"), None, "head"),
        P(("rep", "seq"), "head", None),
        P(("rep", "seq"), "head"),
        P(("rep", "seq"), "head", None),
    )
    return jax.shard_map(shards, mesh=mesh, in_specs=in_specs, out_specs=out_specs, check_vma=False)
```
